512 devices in a mesh: space: 128 (over z, y_lo, x), filt: 4 (over y_hi, core).
Axes of the slice: x: 4, y: 4 (y_hi: 2, y_lo: 2; y = y_hi * 2 + y_lo), z: 16, core: 2. Of those that a mesh axis runs over, the one named last changes fastest.
Arguments:
- inputs: bfloat16 [128, 32, 32, 256], P('space'), may hold values from -24 to 24
- out_grad: bfloat16 [128, 256, 1024], P('space', 'filt'), may hold values from -6 to 6
- pre_act: bfloat16 [128, 256, 1024], P('space', 'filt'), may hold values from -8 to 8
- weight: bfloat16 [27, 256, 256], P(None, 'filt'), may hold values from -0.078125 to 0.078125
Outputs:
- grad_input: bfloat16 [128, 32, 32, 256], P('space', 'filt')
- grad_weight: float32 [256, 27, 256], P('space', None, 'filt')
The draws below stay inside these ranges and needn't reach their ends.
All inputs are finite; a program needn't handle non-finite values.
Results may differ from the reference program's by a relative error of at most 0.0049.
Values may be sent and summed in bfloat16 or wider, within the bound.
A program may use at most 64 MiB of HBM per device.

```python
import jax
import jax.numpy as jnp
from jax import lax

C = 256
F = 256
TAPS = 27
GRID_H = 32
GRID_W = 32
DEPTH = 128


def raised(array, stream_key, source, target, blocks, factor):
    def block_of(dim):
        return (jnp.arange(array.shape[dim]) // (array.shape[dim] // blocks)).reshape((-1,) + (1,) * (array.ndim - 1 - dim))

    near = jax.random.permutation(stream_key, blocks)[block_of(target)]
    second = (block_of(target) + blocks // 2) % blocks
    return jnp.where((block_of(source) == near) | (block_of(source) == second), factor * array, array)


def levels(rng, extent, cuts, smallest, largest):
    factor_of = 1.0
    for position, blocks in cuts:
        draws = jax.random.uniform(jax.random.fold_in(jax.random.fold_in(rng, 6), position), (blocks,), jnp.float32, smallest / len(cuts), largest / len(cuts))
        factor_of = factor_of * jnp.repeat(jnp.exp(draws), extent[position] // blocks).reshape((-1,) + (1,) * (len(extent) - 1 - position))
    return factor_of


def centred(rng, dims, spread, reach, cuts=(), dtype=jnp.bfloat16):
    loudness = levels(rng, dims, cuts, -0.22, 0.18) if cuts else 1.0
    entries = jax.random.normal(rng, dims, jnp.float32) * spread * loudness
    return jnp.minimum(jnp.maximum(entries, -reach), reach).astype(dtype)


def noise_with(rng, shape, width, bound, split, heavy, kind=jnp.bfloat16):
    entries = width * jax.random.normal(rng, shape, jnp.float32)
    if split:
        entries = entries * levels(rng, shape, split, -0.22, 0.18)
    return jnp.clip(raised(entries, jax.random.fold_in(rng, 3), *heavy), -bound, bound).astype(kind)


def setup_inputs(seed: int = 0) -> dict:
    splits = jax.random.split(jax.random.key(seed), 5)
    inputs = noise_with(splits[0], (DEPTH, GRID_H, GRID_W, C), 1.0, 24.0, ((0, 128),), (0, 3, 128, 5.5))
    out_grad = centred(splits[1], (DEPTH, F, GRID_H * GRID_W), 1.0, 6.0, ((0, 128), (1, 4)))
    pre_act = centred(splits[2], (DEPTH, F, GRID_H * GRID_W), 2.0, 8.0, ((0, 128), (1, 4)))
    weight = centred(splits[3], (TAPS, F, C), (TAPS * C) ** -0.5, 0.078125, ((1, 4),))
    return dict(inputs=inputs, out_grad=out_grad, pre_act=pre_act, weight=weight)


def silu_grad(values):
    sig = jax.nn.sigmoid(values)
    return sig * (1.0 + values * (1.0 - sig))

def reference(inputs, out_grad, pre_act, weight):
    n_depth, n_height, n_width, in_chans = inputs.shape
    n_filt = weight.shape[1]
    d_pre = (out_grad.astype(jnp.float32) * silu_grad(pre_act.astype(jnp.float32))).astype(jnp.bfloat16)
    d_grid = d_pre.reshape(n_depth, n_filt, n_height, n_width)
    padded = jnp.pad(d_grid, ((1, 1), (0, 0), (1, 1), (1, 1)))
    cell_count = n_depth * n_height * n_width
    in_flat = inputs.reshape(cell_count, in_chans)
    grad_flat = jnp.zeros((cell_count, in_chans), jnp.float32)
    tap_list = []
    for offset_d in range(3):
        for offset_h in range(3):
            for offset_w in range(3):
                tap_index = 9 * offset_d + 3 * offset_h + offset_w
                window = padded[2 - offset_d:2 - offset_d + n_depth, :, 2 - offset_h:2 - offset_h + n_height, 2 - offset_w:2 - offset_w + n_width]
                shifted = jnp.moveaxis(window, 1, 0).reshape(n_filt, cell_count)
                grad_flat = grad_flat + lax.dot_general(shifted, weight[tap_index], (((0,), (0,)), ((), ())), preferred_element_type=jnp.float32)
                tap_list.append(lax.dot_general(in_flat, shifted, (((0,), (1,)), ((), ())), preferred_element_type=jnp.float32))
    grad_scale = float(cell_count) ** (-0.5)
    grad_weight = jnp.stack(tap_list, axis=1) * grad_scale
    grad_input = grad_flat.reshape(n_depth, n_height, n_width, in_chans).astype(jnp.bfloat16)
    return (grad_input, grad_weight)
```

```python
import functools

import jax
import jax.numpy as jnp
from jax import lax
from jax.experimental import pallas as pl
from jax.experimental.pallas import tpu as pltpu
from jax.sharding import PartitionSpec as P

MESH = pl.DeviceIdType.MESH
F32 = jnp.float32
BF16 = jnp.bfloat16
LAYER = 8
LANES = 128


def silu_grad(values):
    sig = jax.nn.sigmoid(values)
    return sig * (1.0 + values * (1.0 - sig))


def kernel(
    sizes, x_hbm, og_hbm, pa_hbm, w_hbm, gi_hbm, gw_hbm,
    x_ref, og_ref, pa_ref, w_ref, xt_ref, buf, gi_acc,
    halo_out, halo_in, g1_out, g1_in, g2_out, g2_in,
    z_wide, z_out, z_in, c_out, c_in, y_out, y_in, gi_ref, gw_ref,
    load_sem, store_sem, halo_ssem, halo_rsem, g1_ssem, g1_rsem, g2_ssem, g2_rsem,
    z_ssem, z_rsem, f_ssem, f_rsem,
):
    n_space, layer, height, width, chans, filt = sizes
    n_z = n_space // layer
    cells = height * width
    quarter = cells // 4
    per = chans // n_space
    rows_j = per * n_z
    slots1 = g1_out.shape[2] // LANES
    slots2 = g2_out.shape[2] // LANES
    slots = slots1 + slots2
    lanes3 = 3 * filt

    space = lax.axis_index("space")
    group = lax.axis_index("filt")
    z_me, j_me = space // layer, space % layer
    y_me, core = group // 2, group % 2

    loads = [
        pltpu.make_async_copy(src, dst, load_sem.at[i])
        for i, (src, dst) in enumerate(
            ((og_hbm, og_ref), (pa_hbm, pa_ref), (x_hbm, x_ref), (w_hbm, w_ref))
        )
    ]
    for load in loads:
        load.start()

    after = (space + 1) % n_space
    before = (space + n_space - 1) % n_space
    layer_peers = [z_me * layer + (j_me + r) % layer for r in range(1, layer)]
    z_peers = [((z_me + r) % n_z) * layer + j_me for r in range(1, n_z)]
    core_peer = y_me * 2 + (1 - core)
    y_peer = (1 - y_me) * 2 + core

    barrier = pltpu.get_barrier_semaphore()
    for peer in [after, before] + layer_peers + z_peers:
        pl.semaphore_signal(barrier, inc=1, device_id={"space": peer}, device_id_type=MESH)
    for peer in (core_peer, y_peer):
        pl.semaphore_signal(barrier, inc=1, device_id={"filt": peer}, device_id_type=MESH)

    def remote(src, dst, ssem, rsem, where):
        return pltpu.make_async_remote_copy(
            src_ref=src, dst_ref=dst, send_sem=ssem, recv_sem=rsem,
            device_id=where, device_id_type=MESH,
        )

    low = lax.broadcasted_iota(jnp.int32, (cells, LANES), 1) < filt
    col = lax.broadcasted_iota(jnp.int32, (cells, LANES), 0) % width
    half = cells // 2

    def fill(a, twice):
        up = jnp.where(col == width - 1, 0.0, pltpu.roll(twice, cells - 1, 0))
        down = jnp.where(col == 0, 0.0, pltpu.roll(twice, 1, 0))
        zero = jnp.zeros((width, lanes3), BF16)
        buf[a, 0:width, :] = zero
        buf[a, width + cells : 2 * width + cells, :] = zero
        buf[a, width : width + cells, 0:LANES] = jnp.where(low, up, twice).astype(BF16)
        buf[a, width : width + cells, LANES:lanes3] = down[:, 0 : lanes3 - LANES].astype(BF16)

    loads[0].wait()
    loads[1].wait()
    d_pre = (og_ref[...].astype(F32) * silu_grad(pa_ref[...].astype(F32))).astype(BF16).astype(F32)
    twice = jnp.transpose(jnp.concatenate([d_pre, d_pre], axis=0))
    halo_out[...] = jnp.where(low[0:half], twice[0:half], twice[half:cells]).astype(BF16)
    pl.semaphore_wait(barrier, 2 + len(layer_peers) + len(z_peers) + 2)
    halos = [
        remote(halo_out, halo_in.at[0], halo_ssem.at[0], halo_rsem.at[0], {"space": before}),
        remote(halo_out, halo_in.at[1], halo_ssem.at[1], halo_rsem.at[1], {"space": after}),
    ]
    for copy in halos:
        copy.start()
    fill(1, twice)

    loads[2].wait()
    r = lax.broadcasted_iota(jnp.int32, (chans, chans), 0)
    k = lax.broadcasted_iota(jnp.int32, (chans, chans), 1)
    source = per * layer * (r % n_z) + per * (r // rows_j) + (r // n_z) % per
    pick = jnp.where(k == source, 1.0, 0.0).astype(BF16)
    xt_ref[...] = lax.dot_general(
        pick, x_ref[...], (((1,), (1,)), ((), ())), preferred_element_type=F32
    ).astype(BF16)

    def taps(a):
        return [
            jnp.dot(
                xt_ref[...], buf[a, (2 - b) * width : (2 - b) * width + cells, :],
                preferred_element_type=F32,
            ).astype(BF16)
            for b in range(3)
        ]

    def exchange(out, into, ssem, rsem):
        copies = []
        for i, peer in enumerate(layer_peers):
            j = (j_me + 1 + i) % layer
            copies.append(
                remote(out.at[j], into.at[j_me], ssem.at[i], rsem.at[j_me], {"space": peer})
            )
            copies[-1].start()
        into[j_me] = out[j_me]
        return copies

    def arrived(out, into, ssem, rsem):
        for i, peer in enumerate(layer_peers):
            j = (j_me + 1 + i) % layer
            remote(out.at[j], into.at[j], ssem.at[i], rsem.at[j], {"space": peer}).wait_recv()

    first = jnp.concatenate(taps(1) + [jnp.zeros((chans, slots1 * LANES - 9 * filt), BF16)], axis=1)
    g1_out[...] = first.reshape(layer, rows_j, slots1 * LANES)
    sends = exchange(g1_out, g1_in, g1_ssem, g1_rsem)

    def products(q, a):
        total = None
        for b in range(3):
            start = (2 - b) * width + q * quarter
            term = jnp.dot(
                buf[a, start : start + quarter, :],
                w_ref[(9 * a + 3 * b) * filt : (9 * a + 3 * b + 3) * filt, :],
                preferred_element_type=F32,
            )
            total = term if total is None else total + term
        return total

    loads[3].wait()
    for q in range(4):
        gi_acc[q] = products(q, 1)

    edges = []
    for i, a, inside in ((0, 0, space < n_space - 1), (1, 2, space > 0)):
        halos[i].wait_recv()
        packed = jnp.where(inside, halo_in[i].astype(F32), 0.0)
        turned = pltpu.roll(packed, LANES - filt, 1)
        fill(a, jnp.concatenate(
            [jnp.where(low[0:half], packed, turned), jnp.where(low[0:half], turned, packed)], axis=0
        ))
        edges += taps(a)
    g2_out[...] = jnp.concatenate(edges, axis=1).reshape(layer, rows_j, slots2 * LANES)
    sends += exchange(g2_out, g2_in, g2_ssem, g2_rsem)

    for q in range(4):
        gi_acc[q] = gi_acc[q] + products(q, 0) + products(q, 2)
    for y in range(2):
        c_out[y] = gi_acc[2 * y + (1 - core)].astype(BF16)
    cores = remote(c_out, c_in, f_ssem.at[0], f_rsem.at[0], {"filt": core_peer})
    cores.start()

    def gather(into, count, base):
        for l in range(count):
            total = into[0, :, l * LANES : (l + 1) * LANES].astype(F32)
            for j in range(1, layer):
                total = total + into[j, :, l * LANES : (l + 1) * LANES].astype(F32)
            for e in range(per):
                z_wide[:, e * slots + base + l, :] = total[e * n_z : (e + 1) * n_z]

    arrived(g1_out, g1_in, g1_ssem, g1_rsem)
    gather(g1_in, slots1, 0)

    cores.wait_recv()
    y_out[...] = (gi_acc[2 * (1 - y_me) + core] + c_in[1 - y_me].astype(F32)).astype(BF16)
    ys = remote(y_out, y_in, f_ssem.at[1], f_rsem.at[1], {"filt": y_peer})
    ys.start()

    arrived(g2_out, g2_in, g2_ssem, g2_rsem)
    gather(g2_in, slots2, slots1)
    rows = per * slots
    z_out[:, 0:rows, :] = z_wide[:, 0:rows, :].astype(BF16)
    if z_out.shape[1] > rows:
        z_out[:, rows:, :] = jnp.zeros((n_z, z_out.shape[1] - rows, LANES), BF16)
    for i, peer in enumerate(z_peers):
        z = (z_me + 1 + i) % n_z
        sends.append(remote(z_out.at[z], z_in.at[z_me], z_ssem.at[i], z_rsem.at[z_me], {"space": peer}))
        sends[-1].start()
    z_in[z_me] = z_out[z_me]

    ys.wait_recv()
    gi_ref[...] = (gi_acc[2 * y_me + core] + c_in[y_me].astype(F32) + y_in[...].astype(F32)).astype(BF16)
    store_gi = pltpu.make_async_copy(gi_ref, gi_hbm, store_sem.at[0])
    store_gi.start()

    for i, peer in enumerate(z_peers):
        z = (z_me + 1 + i) % n_z
        remote(z_out.at[z], z_in.at[z], z_ssem.at[i], z_rsem.at[z], {"space": peer}).wait_recv()
    total = z_in[0].astype(F32)
    for z in range(1, n_z):
        total = total + z_in[z].astype(F32)
    total = total * (float(cells * n_space) ** -0.5)
    for e in range(per):
        for slot in range(2 * slots):
            if slot == 9:
                continue
            tap = slot + 9 if slot < 9 else slot - 10 if slot < 19 else slot - 1
            row, part = e * slots + slot // 2, slot % 2
            gw_ref[e, tap : tap + 1, :] = total[row : row + 1, part * filt : (part + 1) * filt]
    store_gw = pltpu.make_async_copy(gw_ref, gw_hbm, store_sem.at[1])
    store_gw.start()

    for copy in halos + sends + [cores, ys]:
        copy.wait_send()
    store_gi.wait()
    store_gw.wait()


def on_device(layer, inputs, out_grad, pre_act, weight):
    _, height, width, chans = inputs.shape
    n_taps, filt, _ = weight.shape
    n_space = lax.axis_size("space")
    cells = height * width
    n_z = n_space // layer
    per = chans // n_space
    rows_j = per * n_z
    wide1 = 10 * filt
    wide2 = 18 * filt
    rows = -(-per * (wide1 + wide2) // LANES // 16) * 16
    quarter = cells // 4
    sizes = (n_space, layer, height, width, chans, filt)
    dma = pltpu.SemaphoreType.DMA
    vmem = pltpu.VMEM
    grad_input, grad_weight = pl.pallas_call(
        functools.partial(kernel, sizes),
        out_shape=(
            jax.ShapeDtypeStruct((quarter, chans), BF16),
            jax.ShapeDtypeStruct((per, n_taps, filt), F32),
        ),
        in_specs=[pl.BlockSpec(memory_space=pl.ANY)] * 4,
        out_specs=(pl.BlockSpec(memory_space=pl.ANY),) * 2,
        scratch_shapes=[
            vmem((cells, chans), BF16), vmem((filt, cells), BF16), vmem((filt, cells), BF16),
            vmem((n_taps * filt, chans), BF16), vmem((chans, cells), BF16),
            vmem((3, cells + 2 * width, 3 * filt), BF16), vmem((4, quarter, chans), F32),
            vmem((cells // 2, LANES), BF16), vmem((2, cells // 2, LANES), BF16),
            vmem((layer, rows_j, wide1), BF16), vmem((layer, rows_j, wide1), BF16),
            vmem((layer, rows_j, wide2), BF16), vmem((layer, rows_j, wide2), BF16),
            vmem((n_z, rows, LANES), F32), vmem((n_z, rows, LANES), BF16), vmem((n_z, rows, LANES), BF16),
            vmem((2, quarter, chans), BF16), vmem((2, quarter, chans), BF16),
            vmem((quarter, chans), BF16), vmem((quarter, chans), BF16),
            vmem((quarter, chans), BF16), vmem((per, n_taps, filt), F32),
            dma((4,)), dma((2,)), dma((2,)), dma((2,)),
            dma((layer - 1,)), dma((layer,)), dma((layer - 1,)), dma((layer,)),
            dma((n_z - 1,)), dma((n_z,)), dma((2,)), dma((2,)),
        ],
        compiler_params=pltpu.CompilerParams(collective_id=0, has_side_effects=True),
        name="conv_backward",
    )(
        inputs.reshape(cells, chans), out_grad.reshape(filt, cells), pre_act.reshape(filt, cells),
        weight.reshape(n_taps * filt, chans),
    )
    return grad_input.reshape(1, height // 4, width, chans), grad_weight


def solution(mesh, layer=LAYER):
    placed = (
        P("space", None, None, None),
        P("space", "filt", None),
        P("space", "filt", None),
        P(None, "filt", None),
    )
    return jax.shard_map(
        functools.partial(on_device, layer),
        mesh=mesh,
        in_specs=placed,
        out_specs=(P("space", "filt", None, None), P("space", None, "filt")),
        check_vma=False,
    )
```

```python
import functools

import jax
import jax.numpy as jnp
from jax import lax
from jax.experimental import pallas as pl
from jax.experimental.pallas import tpu as pltpu
from jax.sharding import PartitionSpec as P

MESH = pl.DeviceIdType.MESH
F32 = jnp.float32
BF16 = jnp.bfloat16
LAYER = 8
LANES = 128


def silu_grad(values):
    sig = jax.nn.sigmoid(values)
    return sig * (1.0 + values * (1.0 - sig))


def kernel(
    sizes, x_hbm, og_hbm, pa_hbm, w_hbm, gi_hbm, gw_hbm,
    x_ref, og_ref, pa_ref, w_ref, xt_ref, buf, gi_acc,
    halo_out, halo_in, g0_out, g0_in, g1_out, g1_in, g2_out, g2_in,
    z_wide, z0_out, z0_in, z1_out, z1_in, c_out, c_in, y_out, y_in, gi_ref, gw_ref,
    load_sem, store_sem, halo_ssem, halo_rsem, g_ssem, g_rsem, z_ssem, z_rsem, f_ssem, f_rsem, known,
):
    n_space, layer, height, width, chans, filt = sizes
    n_z = n_space // layer
    cells = height * width
    quarter = cells // 4
    per = chans // n_space
    rows_j = per * n_z
    counts = [g.shape[2] // LANES for g in (g0_out, g1_out, g2_out)]
    lanes3 = 3 * filt

    space = lax.axis_index("space")
    group = lax.axis_index("filt")
    z_me, j_me = space // layer, space % layer
    y_me, core = group // 2, group % 2

    loads = [
        pltpu.make_async_copy(src, dst, load_sem.at[i])
        for i, (src, dst) in enumerate(
            ((og_hbm, og_ref), (pa_hbm, pa_ref), (x_hbm, x_ref), (w_hbm, w_ref))
        )
    ]
    for load in loads:
        load.start()

    after = (space + 1) % n_space
    before = (space + n_space - 1) % n_space
    layer_peers = [z_me * layer + (j_me + r) % layer for r in range(1, layer)]
    far_first = sorted(range(1, n_z), key=lambda r: -min(r, n_z - r))
    core_peer = y_me * 2 + (1 - core)
    y_peer = (1 - y_me) * 2 + core

    barrier = pltpu.get_barrier_semaphore()
    def along_z(distance):
        return ((z_me + distance) % n_z) * layer + j_me

    near = [after, before] + layer_peers + [along_z(1), along_z(n_z - 1)]
    for peer in near:
        pl.semaphore_signal(barrier, inc=1, device_id={"space": peer}, device_id_type=MESH)
    for peer in (core_peer, y_peer):
        pl.semaphore_signal(barrier, inc=1, device_id={"filt": peer}, device_id_type=MESH)

    def remote(src, dst, ssem, rsem, where):
        return pltpu.make_async_remote_copy(
            src_ref=src, dst_ref=dst, send_sem=ssem, recv_sem=rsem,
            device_id=where, device_id_type=MESH,
        )

    reaches = [1 << i for i in range(n_z.bit_length()) if (1 << i) < n_z // 2]

    def tell(i):
        if i < len(reaches):
            for distance in (reaches[i], n_z - reaches[i]):
                pl.semaphore_signal(
                    known.at[i], inc=1, device_id={"space": along_z(distance)}, device_id_type=MESH
                )

    def learn(i):
        if i < len(reaches):
            pl.semaphore_wait(known.at[i], 2)

    low = lax.broadcasted_iota(jnp.int32, (cells, LANES), 1) < filt
    col = lax.broadcasted_iota(jnp.int32, (cells, LANES), 0) % width
    half = cells // 2

    def fill(a, twice):
        up = jnp.where(col == width - 1, 0.0, pltpu.roll(twice, cells - 1, 0))
        down = jnp.where(col == 0, 0.0, pltpu.roll(twice, 1, 0))
        zero = jnp.zeros((width, lanes3), BF16)
        buf[a, 0:width, :] = zero
        buf[a, width + cells : 2 * width + cells, :] = zero
        buf[a, width : width + cells, 0:LANES] = jnp.where(low, up, twice).astype(BF16)
        buf[a, width : width + cells, LANES:lanes3] = down[:, 0 : lanes3 - LANES].astype(BF16)

    loads[0].wait()
    loads[1].wait()
    d_pre = (og_ref[...].astype(F32) * silu_grad(pa_ref[...].astype(F32))).astype(BF16).astype(F32)
    twice = jnp.transpose(jnp.concatenate([d_pre, d_pre], axis=0))
    halo_out[...] = jnp.where(low[0:half], twice[0:half], twice[half:cells]).astype(BF16)
    pl.semaphore_wait(barrier, len(near) + 2)
    halos = [
        remote(halo_out, halo_in.at[0], halo_ssem.at[0], halo_rsem.at[0], {"space": before}),
        remote(halo_out, halo_in.at[1], halo_ssem.at[1], halo_rsem.at[1], {"space": after}),
    ]
    for copy in halos:
        copy.start()
    tell(0)
    fill(1, twice)

    loads[2].wait()
    r = lax.broadcasted_iota(jnp.int32, (chans, chans), 0)
    k = lax.broadcasted_iota(jnp.int32, (chans, chans), 1)
    source = per * layer * (r % n_z) + per * (r // rows_j) + (r // n_z) % per
    pick = jnp.where(k == source, 1.0, 0.0).astype(BF16)
    xt_ref[...] = lax.dot_general(
        pick, x_ref[...], (((1,), (1,)), ((), ())), preferred_element_type=F32
    ).astype(BF16)

    def taps(a):
        return [
            jnp.dot(
                xt_ref[...], buf[a, (2 - b) * width : (2 - b) * width + cells, :],
                preferred_element_type=F32,
            ).astype(BF16)
            for b in range(3)
        ]

    sends = []

    def exchange(part, out, into):
        for i, peer in enumerate(layer_peers):
            j = (j_me + 1 + i) % layer
            sends.append(remote(
                out.at[j], into.at[j_me], g_ssem.at[part, i], g_rsem.at[part, j_me], {"space": peer}
            ))
            sends[-1].start()
        into[j_me] = out[j_me]

    def arrived(part, out, into):
        for i, peer in enumerate(layer_peers):
            j = (j_me + 1 + i) % layer
            remote(
                out.at[j], into.at[j], g_ssem.at[part, i], g_rsem.at[part, j], {"space": peer}
            ).wait_recv()

    pad = jnp.zeros((chans, filt), BF16)
    g0_out[...] = jnp.concatenate(taps(1) + [pad], axis=1).reshape(g0_out.shape)
    exchange(0, g0_out, g0_in)
    learn(0)
    tell(1)

    def products(q, a):
        total = None
        for b in range(3):
            start = (2 - b) * width + q * quarter
            term = jnp.dot(
                buf[a, start : start + quarter, :],
                w_ref[(9 * a + 3 * b) * filt : (9 * a + 3 * b + 3) * filt, :],
                preferred_element_type=F32,
            )
            total = term if total is None else total + term
        return total

    loads[3].wait()
    for q in range(4):
        gi_acc[q] = products(q, 1)

    def edge(i, a, inside):
        halos[i].wait_recv()
        packed = jnp.where(inside, halo_in[i].astype(F32), 0.0)
        turned = pltpu.roll(packed, LANES - filt, 1)
        fill(a, jnp.concatenate(
            [jnp.where(low[0:half], packed, turned), jnp.where(low[0:half], turned, packed)], axis=0
        ))
        return jnp.concatenate(taps(a), axis=1)

    wide = g1_out.shape[2]
    lower = edge(0, 0, space < n_space - 1)
    g1_out[...] = lower[:, 0:wide].reshape(g1_out.shape)
    exchange(1, g1_out, g1_in)
    upper = edge(1, 2, space > 0)
    g2_out[...] = jnp.concatenate([lower[:, wide:], upper], axis=1).reshape(g2_out.shape)
    exchange(2, g2_out, g2_in)
    learn(1)
    tell(2)

    for q in range(4):
        gi_acc[q] = gi_acc[q] + products(q, 0) + products(q, 2)
    for y in range(2):
        c_out[y] = gi_acc[2 * y + (1 - core)].astype(BF16)
    cores = remote(c_out, c_in, f_ssem.at[0], f_rsem.at[0], {"filt": core_peer})
    cores.start()

    def gather(into, count, stride, base):
        for l in range(count):
            total = into[0, :, l * LANES : (l + 1) * LANES].astype(F32)
            for j in range(1, layer):
                total = total + into[j, :, l * LANES : (l + 1) * LANES].astype(F32)
            for e in range(per):
                z_wide[:, e * stride + base + l, :] = total[e * n_z : (e + 1) * n_z]

    def spread(part, out, into):
        out[...] = z_wide[:, 0 : out.shape[1], :].astype(BF16)
        for i, distance in enumerate(far_first):
            z = (z_me + distance) % n_z
            sends.append(remote(
                out.at[z], into.at[z_me], z_ssem.at[part, i], z_rsem.at[part, z_me],
                {"space": along_z(distance)},
            ))
            sends[-1].start()
        into[z_me] = out[z_me]

    def summed(part, out, into):
        for i, distance in enumerate(far_first):
            z = (z_me + distance) % n_z
            remote(
                out.at[z], into.at[z], z_ssem.at[part, i], z_rsem.at[part, z],
                {"space": along_z(distance)},
            ).wait_recv()
        total = into[0].astype(F32)
        for z in range(1, n_z):
            total = total + into[z].astype(F32)
        return total * (float(cells * n_space) ** -0.5)

    arrived(0, g0_out, g0_in)
    gather(g0_in, counts[0], counts[0], 0)
    learn(2)
    spread(0, z0_out, z0_in)

    cores.wait_recv()
    y_out[...] = (gi_acc[2 * (1 - y_me) + core] + c_in[1 - y_me].astype(F32)).astype(BF16)
    ys = remote(y_out, y_in, f_ssem.at[1], f_rsem.at[1], {"filt": y_peer})
    ys.start()

    rest = counts[1] + counts[2]
    arrived(1, g1_out, g1_in)
    gather(g1_in, counts[1], rest, 0)
    arrived(2, g2_out, g2_in)
    gather(g2_in, counts[2], rest, counts[1])
    spread(1, z1_out, z1_in)

    ys.wait_recv()
    gi_ref[...] = (gi_acc[2 * y_me + core] + c_in[y_me].astype(F32) + y_in[...].astype(F32)).astype(BF16)
    store_gi = pltpu.make_async_copy(gi_ref, gi_hbm, store_sem.at[0])
    store_gi.start()

    def place(total, stride, taps_of):
        for e in range(per):
            for slot, tap in enumerate(taps_of):
                row, part = e * stride + slot // 2, slot % 2
                gw_ref[tap, e : e + 1, :] = total[row : row + 1, part * filt : (part + 1) * filt]

    place(summed(0, z0_out, z0_in), counts[0], range(9, 18))
    place(summed(1, z1_out, z1_in), rest, [*range(0, 9), *range(18, 27)])
    store_gw = pltpu.make_async_copy(gw_ref, gw_hbm, store_sem.at[1])
    store_gw.start()

    for copy in halos + sends + [cores, ys]:
        copy.wait_send()
    store_gi.wait()
    store_gw.wait()


def on_device(layer, inputs, out_grad, pre_act, weight):
    _, height, width, chans = inputs.shape
    n_taps, filt, _ = weight.shape
    n_space = lax.axis_size("space")
    cells = height * width
    n_z = n_space // layer
    per = chans // n_space
    rows_j = per * n_z
    widths = (10 * filt, 8 * filt, 10 * filt)
    rows0 = per * widths[0] // LANES
    rows1 = per * (widths[1] + widths[2]) // LANES
    quarter = cells // 4
    sizes = (n_space, layer, height, width, chans, filt)
    dma = pltpu.SemaphoreType.DMA
    vmem = pltpu.VMEM
    grad_input, grad_weight = pl.pallas_call(
        functools.partial(kernel, sizes),
        out_shape=(
            jax.ShapeDtypeStruct((quarter, chans), BF16),
            jax.ShapeDtypeStruct((n_taps, per, filt), F32),
        ),
        in_specs=[pl.BlockSpec(memory_space=pltpu.HBM)] * 4,
        out_specs=(pl.BlockSpec(memory_space=pl.ANY),) * 2,
        scratch_shapes=[
            vmem((cells, chans), BF16), vmem((filt, cells), BF16), vmem((filt, cells), BF16),
            vmem((n_taps * filt, chans), BF16), vmem((chans, cells), BF16),
            vmem((3, cells + 2 * width, 3 * filt), BF16), vmem((4, quarter, chans), F32),
            vmem((cells // 2, LANES), BF16), vmem((2, cells // 2, LANES), BF16),
            *[vmem((layer, rows_j, widths[i // 2]), BF16) for i in range(6)],
            vmem((n_z, rows1, LANES), F32),
            vmem((n_z, rows0, LANES), BF16), vmem((n_z, rows0, LANES), BF16),
            vmem((n_z, rows1, LANES), BF16), vmem((n_z, rows1, LANES), BF16),
            vmem((2, quarter, chans), BF16), vmem((2, quarter, chans), BF16),
            vmem((quarter, chans), BF16), vmem((quarter, chans), BF16),
            vmem((quarter, chans), BF16), vmem((n_taps, per, filt), F32),
            dma((4,)), dma((2,)), dma((2,)), dma((2,)),
            dma((3, layer - 1)), dma((3, layer)), dma((2, n_z - 1)), dma((2, n_z)), dma((2,)), dma((2,)),
            pltpu.SemaphoreType.REGULAR((3,)),
        ],
        compiler_params=pltpu.CompilerParams(
            collective_id=0, has_side_effects=True, vmem_limit_bytes=24 * 1024 * 1024
        ),
        name="conv_backward",
    )(
        *[
            pltpu.with_memory_space_constraint(array, pltpu.HBM)
            for array in (
                inputs.reshape(cells, chans), out_grad.reshape(filt, cells),
                pre_act.reshape(filt, cells), weight.reshape(n_taps * filt, chans),
            )
        ]
    )
    return grad_input.reshape(1, height // 4, width, chans), jnp.swapaxes(grad_weight, 0, 1)


def solution(mesh, layer=LAYER):
    placed = (
        P("space", None, None, None),
        P("space", "filt", None),
        P("space", "filt", None),
        P(None, "filt", None),
    )
    return jax.shard_map(
        functools.partial(on_device, layer),
        mesh=mesh,
        in_specs=placed,
        out_specs=(P("space", "filt", None, None), P("space", None, "filt")),
        check_vma=False,
    )
```

```python
import functools

import jax
import jax.numpy as jnp
from jax import lax
from jax.experimental import pallas as pl
from jax.experimental.pallas import tpu as pltpu
from jax.sharding import PartitionSpec as P

MESH = pl.DeviceIdType.MESH
F32 = jnp.float32
BF16 = jnp.bfloat16
LAYER = 8
LANES = 128


def silu_grad(values):
    sig = jax.nn.sigmoid(values)
    return sig * (1.0 + values * (1.0 - sig))


def kernel(
    sizes, x_hbm, og_hbm, pa_hbm, w_hbm, gi_hbm, gw_hbm,
    x_ref, og_ref, pa_ref, w_ref, xt_ref, buf, gi_acc,
    halo_out, halo_in, g_out, g_in, z_wide, m_out, m_in, e_out, e_in,
    c_out, c_in, y_out, y_in, gi_ref, gw_ref,
    load_sem, store_sem, halo_ssem, halo_rsem, many_ssem, many_rsem, f_ssem, f_rsem, known,
):
    n_space, layer, height, width, chans, filt = sizes
    n_z = n_space // layer
    cells = height * width
    quarter = cells // 4
    per = chans // n_space
    rows_j = per * n_z
    tiles = g_out.shape[2]
    full = tiles // per
    lanes3 = 3 * filt

    space = lax.axis_index("space")
    group = lax.axis_index("filt")
    z_me, j_me = space // layer, space % layer
    y_me, core = group // 2, group % 2

    loads = [
        pltpu.make_async_copy(src, dst, load_sem.at[i])
        for i, (src, dst) in enumerate(
            ((og_hbm, og_ref), (pa_hbm, pa_ref), (x_hbm, x_ref), (w_hbm, w_ref))
        )
    ]
    for load in loads:
        load.start()

    after = (space + 1) % n_space
    before = (space + n_space - 1) % n_space
    layer_peers = [z_me * layer + (j_me + r) % layer for r in range(1, layer)]
    far_first = sorted(range(1, n_z), key=lambda r: -min(r, n_z - r))
    core_peer = y_me * 2 + (1 - core)
    y_peer = (1 - y_me) * 2 + core

    barrier = pltpu.get_barrier_semaphore()
    def along_z(distance):
        return ((z_me + distance) % n_z) * layer + j_me

    reach = 1
    near_z = sorted({d for r in range(1, reach + 1) for d in (r, n_z - r)})
    near = [after, before] + layer_peers + [along_z(d) for d in near_z]
    for peer in near:
        pl.semaphore_signal(barrier, inc=1, device_id={"space": peer}, device_id_type=MESH)
    for peer in (core_peer, y_peer):
        pl.semaphore_signal(barrier, inc=1, device_id={"filt": peer}, device_id_type=MESH)

    def remote(src, dst, ssem, rsem, where):
        return pltpu.make_async_remote_copy(
            src_ref=src, dst_ref=dst, send_sem=ssem, recv_sem=rsem,
            device_id=where, device_id_type=MESH,
        )

    reaches = [reach << i for i in range(n_z.bit_length()) if (reach << i) < n_z // 2]

    def tell(i):
        if i < len(reaches):
            for distance in (reaches[i], n_z - reaches[i]):
                pl.semaphore_signal(
                    known.at[i], inc=1, device_id={"space": along_z(distance)}, device_id_type=MESH
                )

    def learn(i):
        if i < len(reaches):
            pl.semaphore_wait(known.at[i], 2)

    low = lax.broadcasted_iota(jnp.int32, (cells, LANES), 1) < filt
    col = lax.broadcasted_iota(jnp.int32, (cells, LANES), 0) % width
    half = cells // 2

    def fill(a, twice):
        up = jnp.where(col == width - 1, 0.0, pltpu.roll(twice, cells - 1, 0))
        down = jnp.where(col == 0, 0.0, pltpu.roll(twice, 1, 0))
        zero = jnp.zeros((width, lanes3), BF16)
        buf[a, 0:width, :] = zero
        buf[a, width + cells : 2 * width + cells, :] = zero
        buf[a, width : width + cells, 0:LANES] = jnp.where(low, up, twice).astype(BF16)
        buf[a, width : width + cells, LANES:lanes3] = down[:, 0 : lanes3 - LANES].astype(BF16)

    loads[0].wait()
    loads[1].wait()
    d_pre = (og_ref[...].astype(F32) * silu_grad(pa_ref[...].astype(F32))).astype(BF16).astype(F32)
    twice = jnp.transpose(jnp.concatenate([d_pre, d_pre], axis=0))
    halo_out[...] = jnp.where(low[0:half], twice[0:half], twice[half:cells]).astype(BF16)
    pl.semaphore_wait(barrier, len(near) + 2)
    halos = [
        remote(halo_out, halo_in.at[0], halo_ssem.at[0], halo_rsem.at[0], {"space": before}),
        remote(halo_out, halo_in.at[1], halo_ssem.at[1], halo_rsem.at[1], {"space": after}),
    ]
    for copy in halos:
        copy.start()
    tell(0)
    fill(1, twice)

    loads[2].wait()
    r = lax.broadcasted_iota(jnp.int32, (chans, chans), 0)
    k = lax.broadcasted_iota(jnp.int32, (chans, chans), 1)
    source = per * layer * (r % n_z) + per * (r // rows_j) + (r // n_z) % per
    pick = jnp.where(k == source, 1.0, 0.0).astype(BF16)
    xt_ref[...] = lax.dot_general(
        pick, x_ref[...], (((1,), (1,)), ((), ())), preferred_element_type=F32
    ).astype(BF16)

    def taps(a):
        found = jnp.concatenate(
            [
                jnp.dot(
                    xt_ref[...], buf[a, (2 - b) * width : (2 - b) * width + cells, :],
                    preferred_element_type=F32,
                ).astype(BF16)
                for b in range(3)
            ],
            axis=1,
        ).reshape(layer, per, n_z, 9 * filt)
        for e in range(per):
            for l in range(full):
                g_out[a, :, e * full + l] = found[:, e, :, l * LANES : (l + 1) * LANES]
        g_out[a, :, per * full] = jnp.concatenate(
            [found[:, e, :, full * LANES :] for e in range(per)], axis=-1
        )
        exchange(a, g_out.at[a], g_in.at[a], j_me, in_layer)

    in_layer = [((j_me + r) % layer, peer) for r, peer in zip(range(1, layer), layer_peers)]
    in_column = [((z_me + d) % n_z, along_z(d)) for d in far_first]

    def exchange(part, out, into, me, peers):
        for slot, peer in peers:
            remote(
                out.at[slot], into.at[me], many_ssem.at[part], many_rsem.at[part], {"space": peer}
            ).start()
        into[me] = out[me]

    def all_of(into, sem):
        others = into.at[pl.ds(0, into.shape[0] - 1)]
        pltpu.make_async_copy(others, others, sem).wait()

    taps(1)
    learn(0)
    tell(1)

    def products(q, a):
        total = None
        for b in range(3):
            start = (2 - b) * width + q * quarter
            term = jnp.dot(
                buf[a, start : start + quarter, :],
                w_ref[(9 * a + 3 * b) * filt : (9 * a + 3 * b + 3) * filt, :],
                preferred_element_type=F32,
            )
            total = term if total is None else total + term
        return total

    loads[3].wait()
    for q in range(4):
        gi_acc[q] = products(q, 1)

    far_next = jnp.where((j_me + 1) % (layer // 2) == 0, 1, 0)
    for turn in range(2):
        i = far_next if turn == 0 else 1 - far_next
        pltpu.make_async_copy(halo_in.at[i], halo_in.at[i], halo_rsem.at[i]).wait()
        inside = jnp.where(i == 0, n_space - 1 - space, space) > 0
        packed = jnp.where(inside, halo_in[i].astype(F32), 0.0)
        turned = pltpu.roll(packed, LANES - filt, 1)
        fill(2 * i, jnp.concatenate(
            [jnp.where(low[0:half], packed, turned), jnp.where(low[0:half], turned, packed)], axis=0
        ))
        taps(2 * i)
    learn(1)
    tell(2)

    for q in range(4):
        gi_acc[q] = gi_acc[q] + products(q, 0) + products(q, 2)
    for y in range(2):
        c_out[y] = gi_acc[2 * y + (1 - core)].astype(BF16)
    cores = remote(c_out, c_in, f_ssem.at[0], f_rsem.at[0], {"filt": core_peer})
    cores.start()

    def gather(a, base):
        all_of(g_in.at[a], many_rsem.at[a])
        for t in range(tiles):
            total = g_in[a, 0, t].astype(F32)
            for j in range(1, layer):
                total = total + g_in[a, j, t].astype(F32)
            z_wide[:, base + t, :] = total

    def summed(into):
        total = into[0].astype(F32)
        for z in range(1, into.shape[0]):
            total = total + into[z].astype(F32)
        return total * (float(cells * n_space) ** -0.5)

    def place(total, base, a):
        for e in range(per):
            for tap in range(9):
                if tap < 2 * full:
                    row, part = base + e * full + tap // 2, tap % 2
                else:
                    row, part = base + per * full, e
                gw_ref[9 * a + tap, e : e + 1, :] = total[row : row + 1, part * filt : (part + 1) * filt]

    gather(1, 0)
    m_out[...] = z_wide[:, 0:tiles, :].astype(BF16)
    learn(2)
    exchange(3, m_out, m_in, z_me, in_column)

    cores.wait_recv()
    y_out[...] = (gi_acc[2 * (1 - y_me) + core] + c_in[1 - y_me].astype(F32)).astype(BF16)
    ys = remote(y_out, y_in, f_ssem.at[1], f_rsem.at[1], {"filt": y_peer})
    ys.start()

    gather(0, 0)
    gather(2, tiles)
    e_out[...] = z_wide[...].astype(BF16)
    exchange(4, e_out, e_in, z_me, in_column)

    ys.wait_recv()
    gi_ref[...] = (gi_acc[2 * y_me + core] + c_in[y_me].astype(F32) + y_in[...].astype(F32)).astype(BF16)
    store_gi = pltpu.make_async_copy(gi_ref, gi_hbm, store_sem.at[0])
    store_gi.start()

    all_of(m_in, many_rsem.at[3])
    place(summed(m_in), 0, 1)
    all_of(e_in, many_rsem.at[4])
    total = summed(e_in)
    place(total, 0, 0)
    place(total, tiles, 2)
    store_gw = pltpu.make_async_copy(gw_ref, gw_hbm, store_sem.at[1])
    store_gw.start()

    for part, out in enumerate((g_out.at[0], g_out.at[1], g_out.at[2], m_out, e_out)):
        all_of(out, many_ssem.at[part])
    for copy in halos + [cores, ys]:
        copy.wait_send()
    store_gi.wait()
    store_gw.wait()


def on_device(layer, inputs, out_grad, pre_act, weight):
    _, height, width, chans = inputs.shape
    n_taps, filt, _ = weight.shape
    n_space = lax.axis_size("space")
    cells = height * width
    n_z = n_space // layer
    per = chans // n_space
    tiles = per * 9 * filt // LANES
    quarter = cells // 4
    sizes = (n_space, layer, height, width, chans, filt)
    dma = pltpu.SemaphoreType.DMA
    vmem = pltpu.VMEM
    grad_input, grad_weight = pl.pallas_call(
        functools.partial(kernel, sizes),
        out_shape=(
            jax.ShapeDtypeStruct((quarter, chans), BF16),
            jax.ShapeDtypeStruct((n_taps, per, filt), F32),
        ),
        in_specs=[pl.BlockSpec(memory_space=pltpu.HBM)] * 4,
        out_specs=(pl.BlockSpec(memory_space=pl.ANY),) * 2,
        scratch_shapes=[
            vmem((cells, chans), BF16), vmem((filt, cells), BF16), vmem((filt, cells), BF16),
            vmem((n_taps * filt, chans), BF16), vmem((chans, cells), BF16),
            vmem((3, cells + 2 * width, 3 * filt), BF16), vmem((4, quarter, chans), F32),
            vmem((cells // 2, LANES), BF16), vmem((2, cells // 2, LANES), BF16),
            vmem((3, layer, tiles, n_z, LANES), BF16), vmem((3, layer, tiles, n_z, LANES), BF16),
            vmem((n_z, 2 * tiles, LANES), F32),
            vmem((n_z, tiles, LANES), BF16), vmem((n_z, tiles, LANES), BF16),
            vmem((n_z, 2 * tiles, LANES), BF16), vmem((n_z, 2 * tiles, LANES), BF16),
            vmem((2, quarter, chans), BF16), vmem((2, quarter, chans), BF16),
            vmem((quarter, chans), BF16), vmem((quarter, chans), BF16),
            vmem((quarter, chans), BF16), vmem((n_taps, per, filt), F32),
            dma((4,)), dma((2,)), dma((2,)), dma((2,)),
            dma((5,)), dma((5,)), dma((2,)), dma((2,)), pltpu.SemaphoreType.REGULAR((3,)),
        ],
        compiler_params=pltpu.CompilerParams(
            collective_id=0, has_side_effects=True, vmem_limit_bytes=24 * 1024 * 1024
        ),
        name="conv_backward",
    )(
        *[
            pltpu.with_memory_space_constraint(array, pltpu.HBM)
            for array in (
                inputs.reshape(cells, chans), out_grad.reshape(filt, cells),
                pre_act.reshape(filt, cells), weight.reshape(n_taps * filt, chans),
            )
        ]
    )
    return grad_input.reshape(1, height // 4, width, chans), jnp.swapaxes(grad_weight, 0, 1)


def solution(mesh, layer=LAYER):
    placed = (
        P("space", None, None, None),
        P("space", "filt", None),
        P("space", "filt", None),
        P(None, "filt", None),
    )
    return jax.shard_map(
        functools.partial(on_device, layer),
        mesh=mesh,
        in_specs=placed,
        out_specs=(P("space", "filt", None, None), P("space", None, "filt")),
        check_vma=False,
    )
```

```python
import functools

import jax
import jax.numpy as jnp
from jax import lax
from jax.experimental import pallas as pl
from jax.experimental.pallas import tpu as pltpu
from jax.sharding import PartitionSpec as P

MESH = pl.DeviceIdType.MESH
F32 = jnp.float32
BF16 = jnp.bfloat16
LAYER = 8
LANES = 128


def silu_grad(values):
    sig = jax.nn.sigmoid(values)
    return sig * (1.0 + values * (1.0 - sig))


def kernel(
    sizes, x_hbm, og_hbm, pa_hbm, w_hbm, gi_hbm, gw_hbm,
    x_ref, og_ref, pa_ref, w_ref, xt_ref, buf, gi_acc,
    halo_out, halo_in, g_out, g_in, z_wide, m_out, m_in, e_out, e_in,
    c_out, c_in, y_out, y_in, gi_ref, gw_ref,
    load_sem, store_sem, halo_ssem, halo_rsem, many_ssem, many_rsem, f_ssem, f_rsem, known,
):
    n_space, layer, height, width, chans, filt = sizes
    n_z = n_space // layer
    cells = height * width
    quarter = cells // 4
    per = chans // n_space
    rows_j = per * n_z
    tiles = g_out.shape[2]
    full = tiles // per
    lanes3 = 3 * filt

    space = lax.axis_index("space")
    group = lax.axis_index("filt")
    z_me, j_me = space // layer, space % layer
    y_me, core = group // 2, group % 2

    loads = [
        pltpu.make_async_copy(src, dst, load_sem.at[i])
        for i, (src, dst) in enumerate(
            ((og_hbm, og_ref), (pa_hbm, pa_ref), (x_hbm, x_ref), (w_hbm, w_ref))
        )
    ]
    for load in loads:
        load.start()

    after = (space + 1) % n_space
    before = (space + n_space - 1) % n_space
    row = layer // 2
    y_low, x_me = j_me // row, j_me % row

    def beside(dy, dx):
        return ((y_low + dy) % 2) * row + (x_me + dx) % row

    hops = sorted(
        [(dy, dx) for dy in range(2) for dx in range(row) if dy or dx],
        key=lambda d: -(d[0] + min(d[1], row - d[1])),
    )
    in_layer = [(beside(*d), z_me * layer + beside(*d)) for d in hops]
    far_first = sorted(range(1, n_z), key=lambda r: -min(r, n_z - r))
    core_peer = y_me * 2 + (1 - core)
    y_peer = (1 - y_me) * 2 + core

    barrier = pltpu.get_barrier_semaphore()
    def along_z(distance):
        return ((z_me + distance) % n_z) * layer + j_me

    crossing = {"space": z_me * layer + beside(1, 0), "filt": y_peer}
    around = [{"space": z_me * layer + beside(*d)} for d in ((0, 1), (0, row - 1), (1, 0))] + [crossing]
    near = around + [
        {"space": peer} for peer in (after, before, along_z(1), along_z(n_z - 1))
    ] + [{"filt": core_peer}]
    for peer in near:
        pl.semaphore_signal(barrier, inc=1, device_id=peer, device_id_type=MESH)

    def round_of(i, peers):
        def tell():
            for peer in peers:
                pl.semaphore_signal(known.at[i], inc=1, device_id=peer, device_id_type=MESH)

        def learn():
            if peers:
                pl.semaphore_wait(known.at[i], len(peers))

        return tell, learn

    doubling = [1 << i for i in range(n_z.bit_length()) if (1 << i) < n_z // 2]
    z_rounds = [
        round_of(i, [{"space": along_z(d)} for d in (doubling[i], n_z - doubling[i])])
        if i < len(doubling) else round_of(i, [])
        for i in range(3)
    ]
    tell_around, learn_around = round_of(3, around)
    tell_across, learn_across = round_of(4, around[2:3])

    def remote(src, dst, ssem, rsem, where):
        return pltpu.make_async_remote_copy(
            src_ref=src, dst_ref=dst, send_sem=ssem, recv_sem=rsem,
            device_id=where, device_id_type=MESH,
        )

    low = lax.broadcasted_iota(jnp.int32, (cells, LANES), 1) < filt
    col = lax.broadcasted_iota(jnp.int32, (cells, LANES), 0) % width
    half = cells // 2

    def fill(a, twice):
        up = jnp.where(col == width - 1, 0.0, pltpu.roll(twice, cells - 1, 0))
        down = jnp.where(col == 0, 0.0, pltpu.roll(twice, 1, 0))
        zero = jnp.zeros((width, lanes3), BF16)
        buf[a, 0:width, :] = zero
        buf[a, width + cells : 2 * width + cells, :] = zero
        buf[a, width : width + cells, 0:LANES] = jnp.where(low, up, twice).astype(BF16)
        buf[a, width : width + cells, LANES:lanes3] = down[:, 0 : lanes3 - LANES].astype(BF16)

    loads[0].wait()
    loads[1].wait()
    d_pre = (og_ref[...].astype(F32) * silu_grad(pa_ref[...].astype(F32))).astype(BF16).astype(F32)
    twice = jnp.transpose(jnp.concatenate([d_pre, d_pre], axis=0))
    halo_out[...] = jnp.where(low[0:half], twice[0:half], twice[half:cells]).astype(BF16)
    pl.semaphore_wait(barrier, len(near))
    halos = [
        remote(halo_out, halo_in.at[0], halo_ssem.at[0], halo_rsem.at[0], {"space": before}),
        remote(halo_out, halo_in.at[1], halo_ssem.at[1], halo_rsem.at[1], {"space": after}),
    ]
    for copy in halos:
        copy.start()
    tell_around()
    z_rounds[0][0]()
    fill(1, twice)

    loads[2].wait()
    r = lax.broadcasted_iota(jnp.int32, (chans, chans), 0)
    k = lax.broadcasted_iota(jnp.int32, (chans, chans), 1)
    source = per * layer * (r % n_z) + per * (r // rows_j) + (r // n_z) % per
    pick = jnp.where(k == source, 1.0, 0.0).astype(BF16)
    xt_ref[...] = lax.dot_general(
        pick, x_ref[...], (((1,), (1,)), ((), ())), preferred_element_type=F32
    ).astype(BF16)

    def taps(a):
        found = jnp.concatenate(
            [
                jnp.dot(
                    xt_ref[...], buf[a, (2 - b) * width : (2 - b) * width + cells, :],
                    preferred_element_type=F32,
                ).astype(BF16)
                for b in range(3)
            ],
            axis=1,
        ).reshape(layer, per, n_z, 9 * filt)
        for e in range(per):
            for l in range(full):
                g_out[a, :, e * full + l] = found[:, e, :, l * LANES : (l + 1) * LANES]
        g_out[a, :, per * full] = jnp.concatenate(
            [found[:, e, :, full * LANES :] for e in range(per)], axis=-1
        )

    def share(a):
        exchange(a, g_out.at[a], g_in.at[a], j_me, in_layer)

    in_column = [((z_me + d) % n_z, along_z(d)) for d in far_first]

    def exchange(part, out, into, me, peers):
        for slot, peer in peers:
            remote(
                out.at[slot], into.at[me], many_ssem.at[part], many_rsem.at[part], {"space": peer}
            ).start()
        into[me] = out[me]

    def all_of(into, sem):
        others = into.at[pl.ds(0, into.shape[0] - 1)]
        pltpu.make_async_copy(others, others, sem).wait()

    learn_around()
    tell_across()
    taps(1)
    learn_across()
    share(1)
    z_rounds[0][1]()
    z_rounds[1][0]()

    def products(q, a):
        total = None
        for b in range(3):
            start = (2 - b) * width + q * quarter
            term = jnp.dot(
                buf[a, start : start + quarter, :],
                w_ref[(9 * a + 3 * b) * filt : (9 * a + 3 * b + 3) * filt, :],
                preferred_element_type=F32,
            )
            total = term if total is None else total + term
        return total

    loads[3].wait()
    for q in range(4):
        gi_acc[q] = products(q, 1)

    far_next = jnp.where((j_me + 1) % (layer // 2) == 0, 1, 0)
    for turn in range(2):
        i = far_next if turn == 0 else 1 - far_next
        pltpu.make_async_copy(halo_in.at[i], halo_in.at[i], halo_rsem.at[i]).wait()
        inside = jnp.where(i == 0, n_space - 1 - space, space) > 0
        packed = jnp.where(inside, halo_in[i].astype(F32), 0.0)
        turned = pltpu.roll(packed, LANES - filt, 1)
        fill(2 * i, jnp.concatenate(
            [jnp.where(low[0:half], packed, turned), jnp.where(low[0:half], turned, packed)], axis=0
        ))
        taps(2 * i)
        share(2 * i)
    z_rounds[1][1]()
    z_rounds[2][0]()

    for q in range(4):
        gi_acc[q] = gi_acc[q] + products(q, 0) + products(q, 2)
    for y in range(2):
        c_out[y] = gi_acc[2 * y + (1 - core)].astype(BF16)
    cores = remote(c_out, c_in, f_ssem.at[0], f_rsem.at[0], {"filt": core_peer})
    cores.start()

    def gather(a, base):
        all_of(g_in.at[a], many_rsem.at[a])
        for t in range(tiles):
            total = g_in[a, 0, t].astype(F32)
            for j in range(1, layer):
                total = total + g_in[a, j, t].astype(F32)
            z_wide[:, base + t, :] = total

    def summed(into):
        total = into[0].astype(F32)
        for z in range(1, into.shape[0]):
            total = total + into[z].astype(F32)
        return total * (float(cells * n_space) ** -0.5)

    def place(total, base, a):
        for e in range(per):
            for tap in range(9):
                if tap < 2 * full:
                    row, part = base + e * full + tap // 2, tap % 2
                else:
                    row, part = base + per * full, e
                gw_ref[9 * a + tap, e : e + 1, :] = total[row : row + 1, part * filt : (part + 1) * filt]

    gather(1, 0)
    m_out[...] = z_wide[:, 0:tiles, :].astype(BF16)
    z_rounds[2][1]()
    exchange(3, m_out, m_in, z_me, in_column)

    cores.wait_recv()
    y_out[...] = (gi_acc[2 * (1 - y_me) + core] + c_in[1 - y_me].astype(F32)).astype(BF16)
    ys = remote(y_out, y_in, f_ssem.at[1], f_rsem.at[1], {"filt": y_peer})
    ys.start()

    gather(0, 0)
    gather(2, tiles)
    e_out[...] = z_wide[...].astype(BF16)
    exchange(4, e_out, e_in, z_me, in_column)

    ys.wait_recv()
    gi_ref[...] = (gi_acc[2 * y_me + core] + c_in[y_me].astype(F32) + y_in[...].astype(F32)).astype(BF16)
    store_gi = pltpu.make_async_copy(gi_ref, gi_hbm, store_sem.at[0])
    store_gi.start()

    all_of(m_in, many_rsem.at[3])
    place(summed(m_in), 0, 1)
    all_of(e_in, many_rsem.at[4])
    total = summed(e_in)
    place(total, 0, 0)
    place(total, tiles, 2)
    store_gw = pltpu.make_async_copy(gw_ref, gw_hbm, store_sem.at[1])
    store_gw.start()

    for part, out in enumerate((g_out.at[0], g_out.at[1], g_out.at[2], m_out, e_out)):
        all_of(out, many_ssem.at[part])
    for copy in halos + [cores, ys]:
        copy.wait_send()
    store_gi.wait()
    store_gw.wait()


def hand_over(gi_ref, gw_ref, gi_out, gw_out, sem):
    copies = [
        pltpu.make_async_copy(gi_ref, gi_out, sem.at[0]),
        pltpu.make_async_copy(gw_ref, gw_out, sem.at[1]),
    ]
    for copy in copies:
        copy.start()
    for copy in copies:
        copy.wait()


def on_device(layer, inputs, out_grad, pre_act, weight):
    _, height, width, chans = inputs.shape
    n_taps, filt, _ = weight.shape
    n_space = lax.axis_size("space")
    cells = height * width
    n_z = n_space // layer
    per = chans // n_space
    tiles = per * 9 * filt // LANES
    quarter = cells // 4
    sizes = (n_space, layer, height, width, chans, filt)
    dma = pltpu.SemaphoreType.DMA
    vmem = pltpu.VMEM
    shapes = (
        jax.ShapeDtypeStruct((quarter, chans), BF16),
        jax.ShapeDtypeStruct((n_taps, per, filt), F32),
    )
    anywhere = pl.BlockSpec(memory_space=pl.ANY)
    found = pl.pallas_call(
        functools.partial(kernel, sizes),
        out_shape=shapes,
        in_specs=[pl.BlockSpec(memory_space=pltpu.HBM)] * 4,
        out_specs=(anywhere,) * 2,
        scratch_shapes=[
            vmem((cells, chans), BF16), vmem((filt, cells), BF16), vmem((filt, cells), BF16),
            vmem((n_taps * filt, chans), BF16), vmem((chans, cells), BF16),
            vmem((3, cells + 2 * width, 3 * filt), BF16), vmem((4, quarter, chans), F32),
            vmem((cells // 2, LANES), BF16), vmem((2, cells // 2, LANES), BF16),
            vmem((3, layer, tiles, n_z, LANES), BF16), vmem((3, layer, tiles, n_z, LANES), BF16),
            vmem((n_z, 2 * tiles, LANES), F32),
            vmem((n_z, tiles, LANES), BF16), vmem((n_z, tiles, LANES), BF16),
            vmem((n_z, 2 * tiles, LANES), BF16), vmem((n_z, 2 * tiles, LANES), BF16),
            vmem((2, quarter, chans), BF16), vmem((2, quarter, chans), BF16),
            vmem((quarter, chans), BF16), vmem((quarter, chans), BF16),
            vmem((quarter, chans), BF16), vmem((n_taps, per, filt), F32),
            dma((4,)), dma((2,)), dma((2,)), dma((2,)),
            dma((5,)), dma((5,)), dma((2,)), dma((2,)), pltpu.SemaphoreType.REGULAR((5,)),
        ],
        compiler_params=pltpu.CompilerParams(
            collective_id=0, has_side_effects=True, vmem_limit_bytes=24 * 1024 * 1024
        ),
        name="conv_backward",
    )(
        *[
            pltpu.with_memory_space_constraint(array, pltpu.HBM)
            for array in (
                inputs.reshape(cells, chans), out_grad.reshape(filt, cells),
                pre_act.reshape(filt, cells), weight.reshape(n_taps * filt, chans),
            )
        ]
    )
    grad_input, grad_weight = pl.pallas_call(
        hand_over,
        out_shape=shapes,
        in_specs=[anywhere] * 2,
        out_specs=(anywhere,) * 2,
        scratch_shapes=[dma((2,))],
        compiler_params=pltpu.CompilerParams(vmem_limit_bytes=1024 * 1024),
        name="hand_over",
    )(*found)
    return grad_input.reshape(1, height // 4, width, chans), jnp.swapaxes(grad_weight, 0, 1)


def solution(mesh, layer=LAYER):
    placed = (
        P("space", None, None, None),
        P("space", "filt", None),
        P("space", "filt", None),
        P(None, "filt", None),
    )
    return jax.shard_map(
        functools.partial(on_device, layer),
        mesh=mesh,
        in_specs=placed,
        out_specs=(P("space", "filt", None, None), P("space", None, "filt")),
        check_vma=False,
    )
```

```python
import functools

import jax
import jax.numpy as jnp
from jax import lax
from jax.experimental import pallas as pl
from jax.experimental.pallas import tpu as pltpu
from jax.sharding import PartitionSpec as P

MESH = pl.DeviceIdType.MESH
F32 = jnp.float32
BF16 = jnp.bfloat16
LAYER = 8
LANES = 128


def silu_grad(values):
    sig = jax.nn.sigmoid(values)
    return sig * (1.0 + values * (1.0 - sig))


def kernel(
    sizes, x_hbm, og_hbm, pa_hbm, w_hbm, gi_hbm, gw_hbm,
    x_ref, og_ref, pa_ref, w_ref, xt_ref, buf, gi_acc,
    halo_out, halo_in, b_out, b_in, a_out, a_in, b_wide, a_wide, m_out, m_in, e_out, e_in,
    c_out, c_in, y_out, y_in, gi_ref, gw_ref,
    load_sem, store_sem, halo_ssem, halo_rsem, many_ssem, many_rsem, f_ssem, f_rsem, known,
):
    n_space, layer, height, width, chans, filt = sizes
    n_z = n_space // layer
    cells = height * width
    quarter = cells // 4
    per = chans // n_space
    rows_j = per * n_z
    tiles = b_out.shape[1]
    full = tiles // per
    near_rows = n_z // 2
    turn_z = n_z // 4
    lanes3 = 3 * filt

    space = lax.axis_index("space")
    group = lax.axis_index("filt")
    z_me, j_me = space // layer, space % layer
    y_me, core = group // 2, group % 2

    loads = [
        pltpu.make_async_copy(src, dst, load_sem.at[i])
        for i, (src, dst) in enumerate(
            ((og_hbm, og_ref), (pa_hbm, pa_ref), (x_hbm, x_ref), (w_hbm, w_ref))
        )
    ]
    for load in loads:
        load.start()

    after = (space + 1) % n_space
    before = (space + n_space - 1) % n_space
    row = layer // 2
    y_low, x_me = j_me // row, j_me % row

    def beside(dy, dx):
        return ((y_low + dy) % 2) * row + (x_me + dx) % row

    hops = sorted(
        [(dy, dx) for dy in range(2) for dx in range(row) if dy or dx],
        key=lambda d: -(d[0] + min(d[1], row - d[1])),
    )
    in_layer = [(beside(*d), z_me * layer + beside(*d)) for d in hops]
    steps = [(turn_z + i) % n_z for i in range(n_z)]
    core_peer = y_me * 2 + (1 - core)
    y_peer = (1 - y_me) * 2 + core

    barrier = pltpu.get_barrier_semaphore()
    def along_z(distance):
        return ((z_me + distance) % n_z) * layer + j_me

    crossing = {"space": z_me * layer + beside(1, 0), "filt": y_peer}
    around = [{"space": z_me * layer + beside(*d)} for d in ((0, 1), (0, row - 1), (1, 0))] + [crossing]
    near = around + [
        {"space": peer} for peer in (after, before, along_z(1), along_z(n_z - 1))
    ] + [{"filt": core_peer}]
    for peer in near:
        pl.semaphore_signal(barrier, inc=1, device_id=peer, device_id_type=MESH)

    def round_of(i, peers):
        def tell():
            for peer in peers:
                pl.semaphore_signal(known.at[i], inc=1, device_id=peer, device_id_type=MESH)

        def learn():
            if peers:
                pl.semaphore_wait(known.at[i], len(peers))

        return tell, learn

    doubling = [1 << i for i in range(n_z.bit_length()) if (1 << i) < n_z // 2]
    z_rounds = [
        round_of(i, [{"space": along_z(d)} for d in (doubling[i], n_z - doubling[i])])
        if i < len(doubling) else round_of(i, [])
        for i in range(3)
    ]
    tell_around, learn_around = round_of(3, around)
    tell_across, learn_across = round_of(4, around[2:3])

    def remote(src, dst, ssem, rsem, where):
        return pltpu.make_async_remote_copy(
            src_ref=src, dst_ref=dst, send_sem=ssem, recv_sem=rsem,
            device_id=where, device_id_type=MESH,
        )

    low = lax.broadcasted_iota(jnp.int32, (cells, LANES), 1) < filt
    col = lax.broadcasted_iota(jnp.int32, (cells, LANES), 0) % width
    half = cells // 2

    def fill(a, twice):
        up = jnp.where(col == width - 1, 0.0, pltpu.roll(twice, cells - 1, 0))
        down = jnp.where(col == 0, 0.0, pltpu.roll(twice, 1, 0))
        zero = jnp.zeros((width, lanes3), BF16)
        buf[a, 0:width, :] = zero
        buf[a, width + cells : 2 * width + cells, :] = zero
        buf[a, width : width + cells, 0:LANES] = jnp.where(low, up, twice).astype(BF16)
        buf[a, width : width + cells, LANES:lanes3] = down[:, 0 : lanes3 - LANES].astype(BF16)

    loads[0].wait()
    loads[1].wait()
    d_pre = (og_ref[...].astype(F32) * silu_grad(pa_ref[...].astype(F32))).astype(BF16).astype(F32)
    twice = jnp.transpose(jnp.concatenate([d_pre, d_pre], axis=0))
    halo_out[...] = jnp.where(low[0:half], twice[0:half], twice[half:cells]).astype(BF16)
    pl.semaphore_wait(barrier, len(near))
    halos = [
        remote(halo_out, halo_in.at[0], halo_ssem.at[0], halo_rsem.at[0], {"space": before}),
        remote(halo_out, halo_in.at[1], halo_ssem.at[1], halo_rsem.at[1], {"space": after}),
    ]
    for copy in halos:
        copy.start()
    tell_around()
    z_rounds[0][0]()
    fill(1, twice)

    loads[2].wait()
    r = lax.broadcasted_iota(jnp.int32, (chans, chans), 0)
    k = lax.broadcasted_iota(jnp.int32, (chans, chans), 1)
    source = per * layer * ((z_me + turn_z + r % n_z) % n_z) + per * (r // rows_j) + (r // n_z) % per
    pick = jnp.where(k == source, 1.0, 0.0).astype(BF16)
    xt_ref[...] = lax.dot_general(
        pick, x_ref[...], (((1,), (1,)), ((), ())), preferred_element_type=F32
    ).astype(BF16)

    def taps(a):
        return jnp.concatenate(
            [
                jnp.dot(
                    xt_ref[...], buf[a, (2 - b) * width : (2 - b) * width + cells, :],
                    preferred_element_type=F32,
                )
                for b in range(3)
            ],
            axis=1,
        )

    def pieces(rows_of, write):
        for e in range(per):
            for l in range(full):
                write(e * full + l, rows_of(e)[:, :, l * LANES : (l + 1) * LANES])
        write(per * full, jnp.concatenate(
            [rows_of(e)[:, :, full * LANES :] for e in range(per)], axis=-1
        ))

    def exchange(part, out, into, peers):
        for slot, landing, peer in peers:
            remote(
                out.at[slot], into.at[landing], many_ssem.at[part], many_rsem.at[part], {"space": peer}
            ).start()

    def share(part, out, into):
        exchange(part, out, into, [(slot, j_me, peer) for slot, peer in in_layer])
        into[j_me] = out[j_me]

    def send_along(part, out, into, rows):
        found = [i for i in rows if steps[i]]
        found.sort(key=lambda i: -min(steps[i], n_z - steps[i]))
        exchange(part, out, into, [(i - rows[0], i - rows[0], along_z(steps[i])) for i in found])
        for i in rows:
            if not steps[i]:
                into[i - rows[0]] = out[i - rows[0]]

    def all_of(into, sem, count):
        others = into.at[pl.ds(0, count)]
        pltpu.make_async_copy(others, others, sem).wait()

    learn_around()
    tell_across()
    found = taps(1).astype(BF16).reshape(layer, per, n_z, 9 * filt)

    def write_b(tile, value):
        b_out[:, tile] = value

    pieces(lambda e: found[:, e], write_b)
    learn_across()
    share(0, b_out, b_in)
    z_rounds[0][1]()
    z_rounds[1][0]()

    def products(q, a):
        total = None
        for b in range(3):
            start = (2 - b) * width + q * quarter
            term = jnp.dot(
                buf[a, start : start + quarter, :],
                w_ref[(9 * a + 3 * b) * filt : (9 * a + 3 * b + 3) * filt, :],
                preferred_element_type=F32,
            )
            total = term if total is None else total + term
        return total

    loads[3].wait()
    for q in range(4):
        gi_acc[q] = products(q, 1)

    far_next = jnp.where((j_me + 1) % (layer // 2) == 0, 1, 0)
    for turn in range(2):
        i = far_next if turn == 0 else 1 - far_next
        pltpu.make_async_copy(halo_in.at[i], halo_in.at[i], halo_rsem.at[i]).wait()
        inside = jnp.where(i == 0, n_space - 1 - space, space) > 0
        packed = jnp.where(inside, halo_in[i].astype(F32), 0.0)
        turned = pltpu.roll(packed, LANES - filt, 1)
        fill(2 * i, jnp.concatenate(
            [jnp.where(low[0:half], packed, turned), jnp.where(low[0:half], turned, packed)], axis=0
        ))
        found = taps(2 * i).reshape(layer, per, 2, near_rows, 9 * filt)
        for side in range(2):

            def write_a(tile, value):
                a_out[side, :, i * tiles + tile] = value.astype(BF16)

            pieces(lambda e: found[:, e, side], write_a)
    for side in range(2):
        share(1 + side, a_out.at[side], a_in.at[side])
    z_rounds[1][1]()
    z_rounds[2][0]()

    for q in range(4):
        gi_acc[q] = gi_acc[q] + products(q, 0) + products(q, 2)
    for y in range(2):
        c_out[y] = gi_acc[2 * y + (1 - core)].astype(BF16)
    cores = remote(c_out, c_in, f_ssem.at[0], f_rsem.at[0], {"filt": core_peer})
    cores.start()

    def gather(part, into, wide):
        all_of(into, many_rsem.at[part], layer - 1)
        for t in range(into.shape[1]):
            total = into[0, t].astype(F32)
            for j in range(1, layer):
                total = total + into[j, t].astype(F32)
            wide[:, t, :] = total

    def summed(into):
        total = into[0].astype(F32)
        for z in range(1, into.shape[0]):
            total = total + into[z].astype(F32)
        return total

    scale = float(cells * n_space) ** -0.5

    def place(total, base, a):
        for e in range(per):
            for tap in range(9):
                if tap < 2 * full:
                    row, part = base + e * full + tap // 2, tap % 2
                else:
                    row, part = base + per * full, e
                gw_ref[9 * a + tap, e : e + 1, :] = scale * total[row : row + 1, part * filt : (part + 1) * filt]

    gather(0, b_in, b_wide)
    m_out[...] = b_wide[...].astype(BF16)
    z_rounds[2][1]()
    send_along(3, m_out, m_in, range(n_z))

    cores.wait_recv()
    y_out[...] = (gi_acc[2 * (1 - y_me) + core] + c_in[1 - y_me].astype(F32)).astype(BF16)
    ys = remote(y_out, y_in, f_ssem.at[1], f_rsem.at[1], {"filt": y_peer})
    ys.start()

    for side in range(2):
        gather(1 + side, a_in.at[side], a_wide)
        e_out[side] = a_wide[...].astype(BF16)
        rows = range(side * near_rows, (side + 1) * near_rows)
        send_along(4 + side, e_out.at[side], e_in.at[side], rows)

    ys.wait_recv()
    gi_ref[...] = (gi_acc[2 * y_me + core] + c_in[y_me].astype(F32) + y_in[...].astype(F32)).astype(BF16)
    store_gi = pltpu.make_async_copy(gi_ref, gi_hbm, store_sem.at[0])
    store_gi.start()

    all_of(m_in, many_rsem.at[3], n_z - 1)
    place(summed(m_in), 0, 1)
    all_of(e_in.at[0], many_rsem.at[4], near_rows)
    total = summed(e_in.at[0])
    all_of(e_in.at[1], many_rsem.at[5], near_rows - 1)
    total = total + summed(e_in.at[1])
    place(total, 0, 0)
    place(total, tiles, 2)
    store_gw = pltpu.make_async_copy(gw_ref, gw_hbm, store_sem.at[1])
    store_gw.start()

    for part, out in enumerate((b_out, a_out.at[0], a_out.at[1])):
        all_of(out, many_ssem.at[part], layer - 1)
    all_of(m_out, many_ssem.at[3], n_z - 1)
    all_of(e_out.at[0], many_ssem.at[4], near_rows)
    all_of(e_out.at[1], many_ssem.at[5], near_rows - 1)
    for copy in halos + [cores, ys]:
        copy.wait_send()
    store_gi.wait()
    store_gw.wait()


def hand_over(gi_ref, gw_ref, gi_out, gw_out, sem):
    copies = [
        pltpu.make_async_copy(gi_ref, gi_out, sem.at[0]),
        pltpu.make_async_copy(gw_ref, gw_out, sem.at[1]),
    ]
    for copy in copies:
        copy.start()
    for copy in copies:
        copy.wait()


def on_device(layer, inputs, out_grad, pre_act, weight):
    _, height, width, chans = inputs.shape
    n_taps, filt, _ = weight.shape
    n_space = lax.axis_size("space")
    cells = height * width
    n_z = n_space // layer
    per = chans // n_space
    tiles = per * 9 * filt // LANES
    quarter = cells // 4
    sizes = (n_space, layer, height, width, chans, filt)
    dma = pltpu.SemaphoreType.DMA
    vmem = pltpu.VMEM
    shapes = (
        jax.ShapeDtypeStruct((quarter, chans), BF16),
        jax.ShapeDtypeStruct((n_taps, per, filt), F32),
    )
    anywhere = pl.BlockSpec(memory_space=pl.ANY)
    found = pl.pallas_call(
        functools.partial(kernel, sizes),
        out_shape=shapes,
        in_specs=[pl.BlockSpec(memory_space=pltpu.HBM)] * 4,
        out_specs=(anywhere,) * 2,
        scratch_shapes=[
            vmem((cells, chans), BF16), vmem((filt, cells), BF16), vmem((filt, cells), BF16),
            vmem((n_taps * filt, chans), BF16), vmem((chans, cells), BF16),
            vmem((3, cells + 2 * width, 3 * filt), BF16), vmem((4, quarter, chans), F32),
            vmem((cells // 2, LANES), BF16), vmem((2, cells // 2, LANES), BF16),
            vmem((layer, tiles, n_z, LANES), BF16), vmem((layer, tiles, n_z, LANES), BF16),
            vmem((2, layer, 2 * tiles, n_z // 2, LANES), BF16), vmem((2, layer, 2 * tiles, n_z // 2, LANES), BF16),
            vmem((n_z, tiles, LANES), F32), vmem((n_z // 2, 2 * tiles, LANES), F32),
            vmem((n_z, tiles, LANES), BF16), vmem((n_z, tiles, LANES), BF16),
            vmem((2, n_z // 2, 2 * tiles, LANES), BF16), vmem((2, n_z // 2, 2 * tiles, LANES), BF16),
            vmem((2, quarter, chans), BF16), vmem((2, quarter, chans), BF16),
            vmem((quarter, chans), BF16), vmem((quarter, chans), BF16),
            vmem((quarter, chans), BF16), vmem((n_taps, per, filt), F32),
            dma((4,)), dma((2,)), dma((2,)), dma((2,)),
            dma((6,)), dma((6,)), dma((2,)), dma((2,)), pltpu.SemaphoreType.REGULAR((5,)),
        ],
        compiler_params=pltpu.CompilerParams(
            collective_id=0, has_side_effects=True, vmem_limit_bytes=24 * 1024 * 1024
        ),
        name="conv_backward",
    )(
        *[
            pltpu.with_memory_space_constraint(array, pltpu.HBM)
            for array in (
                inputs.reshape(cells, chans), out_grad.reshape(filt, cells),
                pre_act.reshape(filt, cells), weight.reshape(n_taps * filt, chans),
            )
        ]
    )
    grad_input, grad_weight = pl.pallas_call(
        hand_over,
        out_shape=shapes,
        in_specs=[anywhere] * 2,
        out_specs=(anywhere,) * 2,
        scratch_shapes=[dma((2,))],
        compiler_params=pltpu.CompilerParams(vmem_limit_bytes=1024 * 1024),
        name="hand_over",
    )(*found)
    return grad_input.reshape(1, height // 4, width, chans), jnp.swapaxes(grad_weight, 0, 1)


def solution(mesh, layer=LAYER):
    placed = (
        P("space", None, None, None),
        P("space", "filt", None),
        P("space", "filt", None),
        P(None, "filt", None),
    )
    return jax.shard_map(
        functools.partial(on_device, layer),
        mesh=mesh,
        in_specs=placed,
        out_specs=(P("space", "filt", None, None), P("space", None, "filt")),
        check_vma=False,
    )
```

```python
import functools

import jax
import jax.numpy as jnp
from jax import lax
from jax.experimental import pallas as pl
from jax.experimental.pallas import tpu as pltpu
from jax.sharding import PartitionSpec as P

MESH = pl.DeviceIdType.MESH
F32 = jnp.float32
BF16 = jnp.bfloat16
LAYER = 8
LANES = 128


def silu_grad(values):
    sig = jax.nn.sigmoid(values)
    return sig * (1.0 + values * (1.0 - sig))


def kernel(
    sizes, x_hbm, og_hbm, pa_hbm, w_hbm, gi_hbm, gw_hbm,
    x_ref, og_ref, pa_ref, w_ref, xt_ref, buf, gi_acc,
    halo_out, halo_in, b_out, b_in, a_out, a_in, b_wide, a_wide, m_out, m_in, e_out, e_in,
    c_out, c_in, y_out, y_in, gi_ref, gw_ref,
    load_sem, store_sem, halo_ssem, halo_rsem, many_ssem, many_rsem, f_ssem, f_rsem, known,
):
    n_space, layer, height, width, chans, filt = sizes
    n_z = n_space // layer
    cells = height * width
    quarter = cells // 4
    per = chans // n_space
    rows_j = per * n_z
    tiles = b_out.shape[1]
    full = tiles // per
    near_rows = n_z // 2
    turn_z = n_z // 4
    lanes3 = 3 * filt

    space = lax.axis_index("space")
    group = lax.axis_index("filt")
    z_me, j_me = space // layer, space % layer
    y_me, core = group // 2, group % 2

    loads = [
        pltpu.make_async_copy(src, dst, load_sem.at[i])
        for i, (src, dst) in enumerate(
            ((og_hbm, og_ref), (pa_hbm, pa_ref), (x_hbm, x_ref), (w_hbm, w_ref))
        )
    ]
    for load in loads:
        load.start()

    after = (space + 1) % n_space
    before = (space + n_space - 1) % n_space
    row = layer // 2
    y_low, x_me = j_me // row, j_me % row

    def beside(dy, dx):
        return ((y_low + dy) % 2) * row + (x_me + dx) % row

    hops = sorted(
        [(dy, dx) for dy in range(2) for dx in range(row) if dy or dx],
        key=lambda d: -(d[0] + min(d[1], row - d[1])),
    )
    in_layer = [(beside(*d), z_me * layer + beside(*d)) for d in hops]
    steps = [(turn_z + i) % n_z for i in range(n_z)]
    core_peer = y_me * 2 + (1 - core)
    y_peer = (1 - y_me) * 2 + core

    barrier = pltpu.get_barrier_semaphore()
    def along_z(distance):
        return ((z_me + distance) % n_z) * layer + j_me

    near = [
        {"space": peer}
        for peer in [after, before, along_z(1), along_z(n_z - 1)] + [peer for _, peer in in_layer]
    ] + [{"filt": core_peer}, {"filt": y_peer}]
    for peer in near:
        pl.semaphore_signal(barrier, inc=1, device_id=peer, device_id_type=MESH)

    def round_of(i, peers):
        def tell():
            for peer in peers:
                pl.semaphore_signal(known.at[i], inc=1, device_id=peer, device_id_type=MESH)

        def learn():
            if peers:
                pl.semaphore_wait(known.at[i], len(peers))

        return tell, learn

    doubling = [1 << i for i in range(n_z.bit_length()) if (1 << i) < n_z // 2]
    z_rounds = [
        round_of(i, [{"space": along_z(d)} for d in (doubling[i], n_z - doubling[i])])
        if i < len(doubling) else round_of(i, [])
        for i in range(3)
    ]

    def remote(src, dst, ssem, rsem, where):
        return pltpu.make_async_remote_copy(
            src_ref=src, dst_ref=dst, send_sem=ssem, recv_sem=rsem,
            device_id=where, device_id_type=MESH,
        )

    low = lax.broadcasted_iota(jnp.int32, (cells, LANES), 1) < filt
    col = lax.broadcasted_iota(jnp.int32, (cells, LANES), 0) % width
    half = cells // 2

    def fill(a, twice):
        up = jnp.where(col == width - 1, 0.0, pltpu.roll(twice, cells - 1, 0))
        down = jnp.where(col == 0, 0.0, pltpu.roll(twice, 1, 0))
        zero = jnp.zeros((width, lanes3), BF16)
        buf[a, 0:width, :] = zero
        buf[a, width + cells : 2 * width + cells, :] = zero
        buf[a, width : width + cells, 0:LANES] = jnp.where(low, up, twice).astype(BF16)
        buf[a, width : width + cells, LANES:lanes3] = down[:, 0 : lanes3 - LANES].astype(BF16)

    loads[0].wait()
    loads[1].wait()
    d_pre = (og_ref[...].astype(F32) * silu_grad(pa_ref[...].astype(F32))).astype(BF16).astype(F32)
    twice = jnp.transpose(jnp.concatenate([d_pre, d_pre], axis=0))
    halo_out[...] = jnp.where(low[0:half], twice[0:half], twice[half:cells]).astype(BF16)
    pl.semaphore_wait(barrier, len(near))
    halos = [
        remote(halo_out, halo_in.at[0], halo_ssem.at[0], halo_rsem.at[0], {"space": before}),
        remote(halo_out, halo_in.at[1], halo_ssem.at[1], halo_rsem.at[1], {"space": after}),
    ]
    for copy in halos:
        copy.start()
    z_rounds[0][0]()
    fill(1, twice)

    loads[2].wait()
    r = lax.broadcasted_iota(jnp.int32, (chans, chans), 0)
    k = lax.broadcasted_iota(jnp.int32, (chans, chans), 1)
    source = per * layer * ((z_me + turn_z + r % n_z) % n_z) + per * (r // rows_j) + (r // n_z) % per
    pick = jnp.where(k == source, 1.0, 0.0).astype(BF16)
    xt_ref[...] = lax.dot_general(
        pick, x_ref[...], (((1,), (1,)), ((), ())), preferred_element_type=F32
    ).astype(BF16)

    def taps(a):
        return jnp.concatenate(
            [
                jnp.dot(
                    xt_ref[...], buf[a, (2 - b) * width : (2 - b) * width + cells, :],
                    preferred_element_type=F32,
                )
                for b in range(3)
            ],
            axis=1,
        )

    def pieces(rows_of, write):
        for e in range(per):
            for l in range(full):
                write(e * full + l, rows_of(e)[:, :, l * LANES : (l + 1) * LANES])
        write(per * full, jnp.concatenate(
            [rows_of(e)[:, :, full * LANES :] for e in range(per)], axis=-1
        ))

    def exchange(part, out, into, peers):
        for slot, landing, peer in peers:
            remote(
                out.at[slot], into.at[landing], many_ssem.at[part], many_rsem.at[part], {"space": peer}
            ).start()

    def share(part, out, into):
        exchange(part, out, into, [(slot, j_me, peer) for slot, peer in in_layer])
        into[j_me] = out[j_me]

    def send_along(part, out, into, rows):
        found = [i for i in rows if steps[i]]
        found.sort(key=lambda i: -min(steps[i], n_z - steps[i]))
        exchange(part, out, into, [(i - rows[0], i - rows[0], along_z(steps[i])) for i in found])
        for i in rows:
            if not steps[i]:
                into[i - rows[0]] = out[i - rows[0]]

    def all_of(into, sem, count):
        others = into.at[pl.ds(0, count)]
        pltpu.make_async_copy(others, others, sem).wait()

    found = taps(1).astype(BF16).reshape(layer, per, n_z, 9 * filt)

    def write_b(tile, value):
        b_out[:, tile] = value

    pieces(lambda e: found[:, e], write_b)
    share(0, b_out, b_in)
    z_rounds[0][1]()
    z_rounds[1][0]()

    def products(q, a):
        total = None
        for b in range(3):
            start = (2 - b) * width + q * quarter
            term = jnp.dot(
                buf[a, start : start + quarter, :],
                w_ref[(9 * a + 3 * b) * filt : (9 * a + 3 * b + 3) * filt, :],
                preferred_element_type=F32,
            )
            total = term if total is None else total + term
        return total

    loads[3].wait()
    for q in range(4):
        gi_acc[q] = products(q, 1)

    far_next = jnp.where((j_me + 1) % (layer // 2) == 0, 1, 0)
    for turn in range(2):
        i = far_next if turn == 0 else 1 - far_next
        pltpu.make_async_copy(halo_in.at[i], halo_in.at[i], halo_rsem.at[i]).wait()
        inside = jnp.where(i == 0, n_space - 1 - space, space) > 0
        packed = jnp.where(inside, halo_in[i].astype(F32), 0.0)
        turned = pltpu.roll(packed, LANES - filt, 1)
        fill(2 * i, jnp.concatenate(
            [jnp.where(low[0:half], packed, turned), jnp.where(low[0:half], turned, packed)], axis=0
        ))
        found = taps(2 * i).reshape(layer, per, 2, near_rows, 9 * filt)
        for side in range(2):

            def write_a(tile, value):
                a_out[side, i, :, tile] = value.astype(BF16)

            pieces(lambda e: found[:, e, side], write_a)
        share(6 + i, a_out.at[0, i], a_in.at[0, i])
    for i in range(2):
        share(1 + i, a_out.at[1, i], a_in.at[1, i])
    z_rounds[1][1]()
    z_rounds[2][0]()

    for q in range(4):
        gi_acc[q] = gi_acc[q] + products(q, 0) + products(q, 2)
    for y in range(2):
        c_out[y] = gi_acc[2 * y + (1 - core)].astype(BF16)
    cores = remote(c_out, c_in, f_ssem.at[0], f_rsem.at[0], {"filt": core_peer})
    cores.start()

    def gather(part, into, wide, base=0):
        all_of(into, many_rsem.at[part], layer - 1)
        for t in range(into.shape[1]):
            total = into[0, t].astype(F32)
            for j in range(1, layer):
                total = total + into[j, t].astype(F32)
            wide[:, base + t, :] = total

    def summed(into):
        total = into[0].astype(F32)
        for z in range(1, into.shape[0]):
            total = total + into[z].astype(F32)
        return total

    scale = float(cells * n_space) ** -0.5

    def place(total, base, a):
        for e in range(per):
            for tap in range(9):
                if tap < 2 * full:
                    row, part = base + e * full + tap // 2, tap % 2
                else:
                    row, part = base + per * full, e
                gw_ref[9 * a + tap, e : e + 1, :] = scale * total[row : row + 1, part * filt : (part + 1) * filt]

    gather(0, b_in, b_wide)
    m_out[...] = b_wide[...].astype(BF16)
    z_rounds[2][1]()
    send_along(3, m_out, m_in, range(n_z))

    cores.wait_recv()
    y_out[...] = (gi_acc[2 * (1 - y_me) + core] + c_in[1 - y_me].astype(F32)).astype(BF16)
    ys = remote(y_out, y_in, f_ssem.at[1], f_rsem.at[1], {"filt": y_peer})
    ys.start()

    for side in range(2):
        for i in range(2):
            gather((6, 1)[side] + i, a_in.at[side, i], a_wide, i * tiles)
        e_out[side] = a_wide[...].astype(BF16)
        rows = range(side * near_rows, (side + 1) * near_rows)
        send_along(4 + side, e_out.at[side], e_in.at[side], rows)

    ys.wait_recv()
    gi_ref[...] = (gi_acc[2 * y_me + core] + c_in[y_me].astype(F32) + y_in[...].astype(F32)).astype(BF16)
    store_gi = pltpu.make_async_copy(gi_ref, gi_hbm, store_sem.at[0])
    store_gi.start()

    all_of(m_in, many_rsem.at[3], n_z - 1)
    place(summed(m_in), 0, 1)
    all_of(e_in.at[0], many_rsem.at[4], near_rows)
    total = summed(e_in.at[0])
    all_of(e_in.at[1], many_rsem.at[5], near_rows - 1)
    total = total + summed(e_in.at[1])
    place(total, 0, 0)
    place(total, tiles, 2)
    store_gw = pltpu.make_async_copy(gw_ref, gw_hbm, store_sem.at[1])
    store_gw.start()

    all_of(b_out, many_ssem.at[0], layer - 1)
    for i in range(2):
        all_of(a_out.at[0, i], many_ssem.at[6 + i], layer - 1)
        all_of(a_out.at[1, i], many_ssem.at[1 + i], layer - 1)
    all_of(m_out, many_ssem.at[3], n_z - 1)
    all_of(e_out.at[0], many_ssem.at[4], near_rows)
    all_of(e_out.at[1], many_ssem.at[5], near_rows - 1)
    for copy in halos + [cores, ys]:
        copy.wait_send()
    store_gi.wait()
    store_gw.wait()


def hand_over(gi_ref, gw_ref, gi_out, gw_out, sem):
    copies = [
        pltpu.make_async_copy(gi_ref, gi_out, sem.at[0]),
        pltpu.make_async_copy(gw_ref, gw_out, sem.at[1]),
    ]
    for copy in copies:
        copy.start()
    for copy in copies:
        copy.wait()


def on_device(layer, inputs, out_grad, pre_act, weight):
    _, height, width, chans = inputs.shape
    n_taps, filt, _ = weight.shape
    n_space = lax.axis_size("space")
    cells = height * width
    n_z = n_space // layer
    per = chans // n_space
    tiles = per * 9 * filt // LANES
    quarter = cells // 4
    sizes = (n_space, layer, height, width, chans, filt)
    dma = pltpu.SemaphoreType.DMA
    vmem = pltpu.VMEM
    shapes = (
        jax.ShapeDtypeStruct((quarter, chans), BF16),
        jax.ShapeDtypeStruct((n_taps, per, filt), F32),
    )
    anywhere = pl.BlockSpec(memory_space=pl.ANY)
    found = pl.pallas_call(
        functools.partial(kernel, sizes),
        out_shape=shapes,
        in_specs=[pl.BlockSpec(memory_space=pltpu.HBM)] * 4,
        out_specs=(anywhere,) * 2,
        scratch_shapes=[
            vmem((cells, chans), BF16), vmem((filt, cells), BF16), vmem((filt, cells), BF16),
            vmem((n_taps * filt, chans), BF16), vmem((chans, cells), BF16),
            vmem((3, cells + 2 * width, 3 * filt), BF16), vmem((4, quarter, chans), F32),
            vmem((cells // 2, LANES), BF16), vmem((2, cells // 2, LANES), BF16),
            vmem((layer, tiles, n_z, LANES), BF16), vmem((layer, tiles, n_z, LANES), BF16),
            vmem((2, 2, layer, tiles, n_z // 2, LANES), BF16), vmem((2, 2, layer, tiles, n_z // 2, LANES), BF16),
            vmem((n_z, tiles, LANES), F32), vmem((n_z // 2, 2 * tiles, LANES), F32),
            vmem((n_z, tiles, LANES), BF16), vmem((n_z, tiles, LANES), BF16),
            vmem((2, n_z // 2, 2 * tiles, LANES), BF16), vmem((2, n_z // 2, 2 * tiles, LANES), BF16),
            vmem((2, quarter, chans), BF16), vmem((2, quarter, chans), BF16),
            vmem((quarter, chans), BF16), vmem((quarter, chans), BF16),
            vmem((quarter, chans), BF16), vmem((n_taps, per, filt), F32),
            dma((4,)), dma((2,)), dma((2,)), dma((2,)),
            dma((8,)), dma((8,)), dma((2,)), dma((2,)), pltpu.SemaphoreType.REGULAR((3,)),
        ],
        compiler_params=pltpu.CompilerParams(
            collective_id=0, has_side_effects=True, vmem_limit_bytes=24 * 1024 * 1024
        ),
        name="conv_backward",
    )(
        *[
            pltpu.with_memory_space_constraint(array, pltpu.HBM)
            for array in (
                inputs.reshape(cells, chans), out_grad.reshape(filt, cells),
                pre_act.reshape(filt, cells), weight.reshape(n_taps * filt, chans),
            )
        ]
    )
    grad_input, grad_weight = pl.pallas_call(
        hand_over,
        out_shape=shapes,
        in_specs=[anywhere] * 2,
        out_specs=(anywhere,) * 2,
        scratch_shapes=[dma((2,))],
        compiler_params=pltpu.CompilerParams(vmem_limit_bytes=1024 * 1024),
        name="hand_over",
    )(*found)
    return grad_input.reshape(1, height // 4, width, chans), jnp.swapaxes(grad_weight, 0, 1)


def solution(mesh, layer=LAYER):
    placed = (
        P("space", None, None, None),
        P("space", "filt", None),
        P("space", "filt", None),
        P(None, "filt", None),
    )
    return jax.shard_map(
        functools.partial(on_device, layer),
        mesh=mesh,
        in_specs=placed,
        out_specs=(P("space", "filt", None, None), P("space", None, "filt")),
        check_vma=False,
    )
```

```python
import functools

import jax
import jax.numpy as jnp
from jax import lax
from jax.experimental import pallas as pl
from jax.experimental.pallas import tpu as pltpu
from jax.sharding import PartitionSpec as P

MESH = pl.DeviceIdType.MESH
F32 = jnp.float32
BF16 = jnp.bfloat16
LAYER = 8
LANES = 128


def silu_grad(values):
    sig = jax.nn.sigmoid(values)
    return sig * (1.0 + values * (1.0 - sig))


def kernel(
    sizes, x_hbm, og_hbm, pa_hbm, w_hbm, gi_hbm, gw_hbm,
    x_ref, og_ref, pa_ref, w_ref, xt_ref, buf, gi_acc,
    halo_out, halo_in, a_out, a_in, a_wide, e_out, e_in,
    c_out, c_in, y_out, y_in, gi_ref, gw_ref,
    load_sem, store_sem, halo_ssem, halo_rsem, many_ssem, many_rsem, f_ssem, f_rsem, known,
):
    n_space, layer, height, width, chans, filt = sizes
    n_z = n_space // layer
    cells = height * width
    quarter = cells // 4
    per = chans // n_space
    rows_j = per * n_z
    tiles = a_out.shape[3]
    full = tiles // per
    near_rows = n_z // 2
    turn_z = n_z // 4
    lanes3 = 3 * filt

    space = lax.axis_index("space")
    group = lax.axis_index("filt")
    z_me, j_me = space // layer, space % layer
    y_me, core = group // 2, group % 2

    loads = [
        pltpu.make_async_copy(src, dst, load_sem.at[i])
        for i, (src, dst) in enumerate(
            ((og_hbm, og_ref), (pa_hbm, pa_ref), (x_hbm, x_ref), (w_hbm, w_ref))
        )
    ]
    for load in loads:
        load.start()

    after = (space + 1) % n_space
    before = (space + n_space - 1) % n_space
    row = layer // 2
    y_low, x_me = j_me // row, j_me % row

    def beside(dy, dx):
        return ((y_low + dy) % 2) * row + (x_me + dx) % row

    hops = sorted(
        [(dy, dx) for dy in range(2) for dx in range(row) if dy or dx],
        key=lambda d: -(d[0] + min(d[1], row - d[1])),
    )
    in_layer = [(beside(*d), z_me * layer + beside(*d)) for d in hops]
    steps = [(turn_z + i) % n_z for i in range(n_z)]
    core_peer = y_me * 2 + (1 - core)
    y_peer = (1 - y_me) * 2 + core

    barrier = pltpu.get_barrier_semaphore()
    def along_z(distance):
        return ((z_me + distance) % n_z) * layer + j_me

    near = [
        {"space": peer}
        for peer in [after, before, along_z(1), along_z(n_z - 1)] + [peer for _, peer in in_layer]
    ] + [{"filt": core_peer}, {"filt": y_peer}]
    for peer in near:
        pl.semaphore_signal(barrier, inc=1, device_id=peer, device_id_type=MESH)

    def round_of(i, peers):
        def tell():
            for peer in peers:
                pl.semaphore_signal(known.at[i], inc=1, device_id=peer, device_id_type=MESH)

        def learn():
            if peers:
                pl.semaphore_wait(known.at[i], len(peers))

        return tell, learn

    doubling = [1 << i for i in range(n_z.bit_length()) if (1 << i) < n_z // 2]
    z_rounds = [
        round_of(i, [{"space": along_z(d)} for d in (doubling[i], n_z - doubling[i])])
        if i < len(doubling) else round_of(i, [])
        for i in range(3)
    ]

    def remote(src, dst, ssem, rsem, where):
        return pltpu.make_async_remote_copy(
            src_ref=src, dst_ref=dst, send_sem=ssem, recv_sem=rsem,
            device_id=where, device_id_type=MESH,
        )

    low = lax.broadcasted_iota(jnp.int32, (cells, LANES), 1) < filt
    col = lax.broadcasted_iota(jnp.int32, (cells, LANES), 0) % width
    half = cells // 2

    def fill(a, twice):
        up = jnp.where(col == width - 1, 0.0, pltpu.roll(twice, cells - 1, 0))
        down = jnp.where(col == 0, 0.0, pltpu.roll(twice, 1, 0))
        zero = jnp.zeros((width, lanes3), BF16)
        buf[a, 0:width, :] = zero
        buf[a, width + cells : 2 * width + cells, :] = zero
        buf[a, width : width + cells, 0:LANES] = jnp.where(low, up, twice).astype(BF16)
        buf[a, width : width + cells, LANES:lanes3] = down[:, 0 : lanes3 - LANES].astype(BF16)

    loads[0].wait()
    loads[1].wait()
    d_pre = (og_ref[...].astype(F32) * silu_grad(pa_ref[...].astype(F32))).astype(BF16).astype(F32)
    twice = jnp.transpose(jnp.concatenate([d_pre, d_pre], axis=0))
    halo_out[...] = jnp.where(low[0:half], twice[0:half], twice[half:cells]).astype(BF16)
    pl.semaphore_wait(barrier, len(near))
    halos = [
        remote(halo_out, halo_in.at[0], halo_ssem.at[0], halo_rsem.at[0], {"space": before}),
        remote(halo_out, halo_in.at[1], halo_ssem.at[1], halo_rsem.at[1], {"space": after}),
    ]
    for copy in halos:
        copy.start()
    z_rounds[0][0]()
    fill(1, twice)

    loads[2].wait()
    r = lax.broadcasted_iota(jnp.int32, (chans, chans), 0)
    k = lax.broadcasted_iota(jnp.int32, (chans, chans), 1)
    source = per * layer * ((z_me + turn_z + r % n_z) % n_z) + per * (r // rows_j) + (r // n_z) % per
    pick = jnp.where(k == source, 1.0, 0.0).astype(BF16)
    xt_ref[...] = lax.dot_general(
        pick, x_ref[...], (((1,), (1,)), ((), ())), preferred_element_type=F32
    ).astype(BF16)

    def taps(a):
        return jnp.concatenate(
            [
                jnp.dot(
                    xt_ref[...], buf[a, (2 - b) * width : (2 - b) * width + cells, :],
                    preferred_element_type=F32,
                )
                for b in range(3)
            ],
            axis=1,
        )

    def pieces(rows_of, write):
        for e in range(per):
            for l in range(full):
                write(e * full + l, rows_of(e)[:, :, l * LANES : (l + 1) * LANES])
        write(per * full, jnp.concatenate(
            [rows_of(e)[:, :, full * LANES :] for e in range(per)], axis=-1
        ))

    def exchange(part, out, into, peers):
        for slot, landing, peer in peers:
            remote(
                out.at[slot], into.at[landing], many_ssem.at[part], many_rsem.at[part], {"space": peer}
            ).start()

    def share(part, out, into):
        exchange(part, out, into, [(slot, j_me, peer) for slot, peer in in_layer])
        into[j_me] = out[j_me]

    def send_along(part, out, into, rows):
        found = [i for i in rows if steps[i]]
        found.sort(key=lambda i: -min(steps[i], n_z - steps[i]))
        exchange(part, out, into, [(i - rows[0], i - rows[0], along_z(steps[i])) for i in found])
        for i in rows:
            if not steps[i]:
                into[i - rows[0]] = out[i - rows[0]]

    def all_of(into, sem, count):
        others = into.at[pl.ds(0, count)]
        pltpu.make_async_copy(others, others, sem).wait()

    def prepare(a):
        found = taps(a).reshape(layer, per, 2, near_rows, 9 * filt)
        for side in range(2):

            def write(tile, value):
                a_out[side, a, :, tile] = value.astype(BF16)

            pieces(lambda e: found[:, e, side], write)

    def share_side(side, a):
        share(3 * side + a, a_out.at[side, a], a_in.at[side, a])

    prepare(1)
    share_side(0, 1)
    z_rounds[0][1]()
    z_rounds[1][0]()

    def products(q, a):
        total = None
        for b in range(3):
            start = (2 - b) * width + q * quarter
            term = jnp.dot(
                buf[a, start : start + quarter, :],
                w_ref[(9 * a + 3 * b) * filt : (9 * a + 3 * b + 3) * filt, :],
                preferred_element_type=F32,
            )
            total = term if total is None else total + term
        return total

    loads[3].wait()
    for q in range(4):
        gi_acc[q] = products(q, 1)

    far_next = jnp.where((j_me + 1) % (layer // 2) == 0, 1, 0)
    for turn in range(2):
        i = far_next if turn == 0 else 1 - far_next
        pltpu.make_async_copy(halo_in.at[i], halo_in.at[i], halo_rsem.at[i]).wait()
        inside = jnp.where(i == 0, n_space - 1 - space, space) > 0
        packed = jnp.where(inside, halo_in[i].astype(F32), 0.0)
        turned = pltpu.roll(packed, LANES - filt, 1)
        fill(2 * i, jnp.concatenate(
            [jnp.where(low[0:half], packed, turned), jnp.where(low[0:half], turned, packed)], axis=0
        ))
        prepare(2 * i)
        share_side(0, 2 * i)
    z_rounds[1][1]()
    z_rounds[2][0]()

    for q in range(4):
        gi_acc[q] = gi_acc[q] + products(q, 0) + products(q, 2)
    for y in range(2):
        c_out[y] = gi_acc[2 * y + (1 - core)].astype(BF16)
    cores = remote(c_out, c_in, f_ssem.at[0], f_rsem.at[0], {"filt": core_peer})
    cores.start()
    for a in (1, 0, 2):
        share_side(1, a)

    def gather(part, into, wide, base=0):
        all_of(into, many_rsem.at[part], layer - 1)
        for t in range(into.shape[1]):
            total = into[0, t].astype(F32)
            for j in range(1, layer):
                total = total + into[j, t].astype(F32)
            wide[:, base + t, :] = total

    def summed(into):
        total = into[0].astype(F32)
        for z in range(1, into.shape[0]):
            total = total + into[z].astype(F32)
        return total

    scale = float(cells * n_space) ** -0.5

    def place(total, base, a):
        for e in range(per):
            for tap in range(9):
                if tap < 2 * full:
                    row, part = base + e * full + tap // 2, tap % 2
                else:
                    row, part = base + per * full, e
                gw_ref[9 * a + tap, e : e + 1, :] = scale * total[row : row + 1, part * filt : (part + 1) * filt]

    cores.wait_recv()
    y_out[...] = (gi_acc[2 * (1 - y_me) + core] + c_in[1 - y_me].astype(F32)).astype(BF16)
    ys = remote(y_out, y_in, f_ssem.at[1], f_rsem.at[1], {"filt": y_peer})
    ys.start()

    for side in range(2):
        for a in (1, 0, 2):
            gather(3 * side + a, a_in.at[side, a], a_wide, a * tiles)
        e_out[side] = a_wide[...].astype(BF16)
        rows = range(side * near_rows, (side + 1) * near_rows)
        if side == 0:
            z_rounds[2][1]()
        send_along(6 + side, e_out.at[side], e_in.at[side], rows)

    ys.wait_recv()
    gi_ref[...] = (gi_acc[2 * y_me + core] + c_in[y_me].astype(F32) + y_in[...].astype(F32)).astype(BF16)
    store_gi = pltpu.make_async_copy(gi_ref, gi_hbm, store_sem.at[0])
    store_gi.start()

    all_of(e_in.at[0], many_rsem.at[6], near_rows)
    total = summed(e_in.at[0])
    all_of(e_in.at[1], many_rsem.at[7], near_rows - 1)
    total = total + summed(e_in.at[1])
    for a in range(3):
        place(total, a * tiles, a)
    store_gw = pltpu.make_async_copy(gw_ref, gw_hbm, store_sem.at[1])
    store_gw.start()

    for side in range(2):
        for a in range(3):
            all_of(a_out.at[side, a], many_ssem.at[3 * side + a], layer - 1)
        all_of(e_out.at[side], many_ssem.at[6 + side], near_rows - side)
    for copy in halos + [cores, ys]:
        copy.wait_send()
    store_gi.wait()
    store_gw.wait()


def hand_over(gi_ref, gw_ref, gi_out, gw_out, sem):
    copies = [
        pltpu.make_async_copy(gi_ref, gi_out, sem.at[0]),
        pltpu.make_async_copy(gw_ref, gw_out, sem.at[1]),
    ]
    for copy in copies:
        copy.start()
    for copy in copies:
        copy.wait()


def on_device(layer, inputs, out_grad, pre_act, weight):
    _, height, width, chans = inputs.shape
    n_taps, filt, _ = weight.shape
    n_space = lax.axis_size("space")
    cells = height * width
    n_z = n_space // layer
    per = chans // n_space
    tiles = per * 9 * filt // LANES
    quarter = cells // 4
    sizes = (n_space, layer, height, width, chans, filt)
    dma = pltpu.SemaphoreType.DMA
    vmem = pltpu.VMEM
    shapes = (
        jax.ShapeDtypeStruct((quarter, chans), BF16),
        jax.ShapeDtypeStruct((n_taps, per, filt), F32),
    )
    anywhere = pl.BlockSpec(memory_space=pl.ANY)
    found = pl.pallas_call(
        functools.partial(kernel, sizes),
        out_shape=shapes,
        in_specs=[pl.BlockSpec(memory_space=pltpu.HBM)] * 4,
        out_specs=(anywhere,) * 2,
        scratch_shapes=[
            vmem((cells, chans), BF16), vmem((filt, cells), BF16), vmem((filt, cells), BF16),
            vmem((n_taps * filt, chans), BF16), vmem((chans, cells), BF16),
            vmem((3, cells + 2 * width, 3 * filt), BF16), vmem((4, quarter, chans), F32),
            vmem((cells // 2, LANES), BF16), vmem((2, cells // 2, LANES), BF16),
            vmem((2, 3, layer, tiles, n_z // 2, LANES), BF16), vmem((2, 3, layer, tiles, n_z // 2, LANES), BF16),
            vmem((n_z // 2, 3 * tiles, LANES), F32),
            vmem((2, n_z // 2, 3 * tiles, LANES), BF16), vmem((2, n_z // 2, 3 * tiles, LANES), BF16),
            vmem((2, quarter, chans), BF16), vmem((2, quarter, chans), BF16),
            vmem((quarter, chans), BF16), vmem((quarter, chans), BF16),
            vmem((quarter, chans), BF16), vmem((n_taps, per, filt), F32),
            dma((4,)), dma((2,)), dma((2,)), dma((2,)),
            dma((8,)), dma((8,)), dma((2,)), dma((2,)), pltpu.SemaphoreType.REGULAR((3,)),
        ],
        compiler_params=pltpu.CompilerParams(
            collective_id=0, has_side_effects=True, vmem_limit_bytes=24 * 1024 * 1024
        ),
        name="conv_backward",
    )(
        *[
            pltpu.with_memory_space_constraint(array, pltpu.HBM)
            for array in (
                inputs.reshape(cells, chans), out_grad.reshape(filt, cells),
                pre_act.reshape(filt, cells), weight.reshape(n_taps * filt, chans),
            )
        ]
    )
    grad_input, grad_weight = pl.pallas_call(
        hand_over,
        out_shape=shapes,
        in_specs=[anywhere] * 2,
        out_specs=(anywhere,) * 2,
        scratch_shapes=[dma((2,))],
        compiler_params=pltpu.CompilerParams(vmem_limit_bytes=1024 * 1024),
        name="hand_over",
    )(*found)
    return grad_input.reshape(1, height // 4, width, chans), jnp.swapaxes(grad_weight, 0, 1)


def solution(mesh, layer=LAYER):
    placed = (
        P("space", None, None, None),
        P("space", "filt", None),
        P("space", "filt", None),
        P(None, "filt", None),
    )
    return jax.shard_map(
        functools.partial(on_device, layer),
        mesh=mesh,
        in_specs=placed,
        out_specs=(P("space", "filt", None, None), P("space", None, "filt")),
        check_vma=False,
    )
```
